32 devices in a mesh: parts: 2 (over x), seq: 8 (over z, y), tensor: 2 (over core).
Axes of the slice: x: 2, y: 2, z: 4, core: 2. Of those that a mesh axis runs over, the one named last changes fastest.
Arguments:
- queries: bfloat16 [3072, 2048], P(('parts', 'seq'), 'tensor'), parts along dimension 0, may hold values from -6 to 6
- key_vectors: bfloat16 [3072, 2048], P(('parts', 'seq'), 'tensor'), parts along dimension 0, may hold values from -6 to 6
- values: bfloat16 [3072, 2048], P(('parts', 'seq'), 'tensor'), parts along dimension 0, may hold values from -150 to 150
- out_weight: bfloat16 [2048, 2048], P('tensor'), may hold values from -0.125 to 0.125
- norm_gain: float32 [2048], P('tensor'), may hold values from 0.1 to 1.9
- grad_output: bfloat16 [3072, 2048], P(('parts', 'seq'), 'tensor'), parts along dimension 0, may hold values from -18 to 18
Outputs:
- mixed: bfloat16 [3072, 2048], P(('parts', 'seq'), 'tensor'), parts along dimension 0
- grad_queries: bfloat16 [3072, 2048], P(('parts', 'seq'), 'tensor'), parts along dimension 0
- grad_keys: bfloat16 [3072, 2048], P(('parts', 'seq'), 'tensor'), parts along dimension 0
- grad_values: bfloat16 [3072, 2048], P(('parts', 'seq'), 'tensor'), parts along dimension 0
- grad_gain: float32 [4096], P(('parts', 'tensor')), parts along dimension 0
The draws below stay inside these ranges and needn't reach their ends.
There are 2 independent parts, one for each index of `parts`. The reference program is written for one: setup_inputs(seed, part) draws one part's arguments, and reference() takes and returns one part's arrays. A program takes and returns all parts, laid end to end along the dimension named above; an argument that names none is the same for every part. Nothing has to cross between parts.
All inputs are finite; a program needn't handle non-finite values.
Results may differ from the reference program's by a relative error of at most 0.018.
Values may be sent and summed in bfloat16 or wider, within the bound.
No kernel may reach another device: no remote copies, remote signals or barrier semaphores. Data moves between devices by JAX's collectives and lax.ppermute only.
A program may use at most 128 MiB of HBM per device.

```python
import math
import jax
import jax.numpy as jnp
from jax import lax

D = 2048
HEADS = 16
DH = 128
TOK_DEV = 192
TOKENS = 1536


def draw_values(key, part):
    first, second, third = jax.random.split(jax.random.fold_in(key, 11), 3)
    base = jax.random.truncated_normal(first, -6.0, 6.0, (TOKENS, D), jnp.float32)
    row_spread = math.log(10.0)
    column_scale = jnp.exp(jax.random.uniform(second, (1, D), jnp.float32, 0.0, math.log(10.0)))
    row_scale = jnp.exp(jax.random.uniform(third, (TOKENS, 1), jnp.float32, 0.0, row_spread))
    return (base * column_scale * row_scale / 4.0).astype(jnp.bfloat16)


def draw_grad_output(key, part):
    first = jax.random.fold_in(key, 23)
    position = jnp.arange(TOKENS).astype(jnp.float32)[:, None] / float(max(TOKENS - 1, 1))
    base = jax.random.truncated_normal(first, -6.0, 6.0, (TOKENS, D), jnp.float32)
    result = base * (1.0 + 2.0 * position)
    return result.astype(jnp.bfloat16)


def level_of(own_key, shape, shards, smallest, largest):
    def one(dim, shards_of):
        draws = jax.random.uniform(jax.random.fold_in(jax.random.fold_in(own_key, 6), dim), (shards_of,), jnp.float32, smallest / len(shards), largest / len(shards))
        return jnp.repeat(jnp.exp(draws), shape[dim] // shards_of).reshape((-1,) + (1,) * (len(shape) - dim - 1))

    factor_of = one(*shards[0])
    for cut in shards[1:]:
        factor_of = factor_of * one(*cut)
    return factor_of


def normal_values(rng, dims, scale, limit, shards=(), dtype=jnp.bfloat16):
    entries = jax.random.normal(rng, dims, jnp.float32) * scale
    if len(shards) > 0:
        entries = level_of(rng, dims, shards, -0.22, 0.18) * entries
    return jnp.clip(entries, min=-limit, max=limit).astype(dtype)


def setup_inputs(seed: int = 0, part: int = 0) -> dict:
    streams_of = jax.random.split(jax.random.key(seed), 7)
    part_keys = jax.random.split(jax.random.fold_in(streams_of[6], part), 7)
    queries = normal_values(part_keys[0], (TOKENS, D), 1.0, 6.0, ((0, 8), (1, 2)))
    key_vectors = normal_values(part_keys[1], (TOKENS, D), 1.0, 6.0, ((0, 8), (1, 2)))
    values = draw_values(jax.random.fold_in(jax.random.fold_in(streams_of[6], part), 71), part)
    out_weight = normal_values(streams_of[3], (D, D), D ** -0.5, 0.125, ((0, 2),))
    norm_gain = jnp.clip(1.0 + 0.18 * jax.random.normal(streams_of[4], (D,), jnp.float32), 0.1, 1.9)
    grad_output = draw_grad_output(jax.random.fold_in(jax.random.fold_in(streams_of[6], part), 71), part)
    return dict(queries=queries, key_vectors=key_vectors, values=values, out_weight=out_weight, norm_gain=norm_gain, grad_output=grad_output)


epsilon = 1e-05
highest = lax.Precision.HIGHEST

def lower_mask(tokens):
    positions = jnp.arange(tokens)
    return positions[:, None] >= positions[None, :]

def forward_block(items):
    query_block, key_block, value_block, prefix_block = items
    causal = lower_mask(query_block.shape[0])[None]
    query_wide = query_block.astype(jnp.float32)
    scores = jnp.einsum('thd,shd->hts', query_wide, key_block.astype(jnp.float32), precision=highest)
    block_scores = jnp.where(causal, scores, 0.0).astype(jnp.bfloat16)
    attention = jnp.einsum('hts,she->the', block_scores.astype(jnp.float32), value_block.astype(jnp.float32), precision=highest)
    attention = attention + jnp.einsum('thd,hde->the', query_wide, prefix_block, precision=highest)
    inverse_rms = lax.rsqrt(lax.optimization_barrier(jnp.mean(attention * attention, axis=-1, keepdims=True)) + epsilon)
    return (attention, inverse_rms)

def backward_block(items):
    query_block, key_block, value_block, prefix_block, suffix_block, grad_attention = items
    causal = lower_mask(query_block.shape[0])[None]
    query_wide = query_block.astype(jnp.float32)
    key_wide = key_block.astype(jnp.float32)
    value_wide = value_block.astype(jnp.float32)
    scores = jnp.einsum('thd,shd->hts', query_wide, key_wide, precision=highest)
    block_scores = jnp.where(causal, scores, 0.0).astype(jnp.bfloat16).astype(jnp.float32)
    grad_low = grad_attention.astype(jnp.bfloat16).astype(jnp.float32)
    grad_raw = jnp.einsum('the,she->hts', grad_low, value_wide, precision=highest)
    grad_scores = jnp.where(causal, grad_raw, 0.0).astype(jnp.bfloat16).astype(jnp.float32)
    grad_queries = jnp.einsum('hts,shd->thd', grad_scores, key_wide, precision=highest)
    grad_queries = grad_queries + jnp.einsum('the,hde->thd', grad_attention, prefix_block, precision=highest)
    grad_keys = jnp.einsum('hts,thd->shd', grad_scores, query_wide, precision=highest)
    grad_keys = grad_keys + jnp.einsum('she,hde->shd', value_wide, suffix_block, precision=highest)
    grad_values = jnp.einsum('hts,the->she', block_scores, grad_low, precision=highest)
    grad_values = grad_values + jnp.einsum('shd,hde->she', key_wide, suffix_block, precision=highest)
    return (grad_queries.astype(jnp.bfloat16), grad_keys.astype(jnp.bfloat16), grad_values.astype(jnp.bfloat16))

def reference(queries, key_vectors, values, out_weight, norm_gain, grad_output):
    blocks = TOKENS // TOK_DEV

    def split(array):
        return array.reshape(blocks, TOK_DEV, HEADS, DH)
    query_blocks = split(queries)
    key_blocks = split(key_vectors)
    value_blocks = split(values)
    gain_heads = norm_gain.reshape(HEADS, DH).astype(jnp.float32)
    local_states = jnp.einsum('bthd,bthe->bhde', key_blocks.astype(jnp.float32), value_blocks.astype(jnp.float32), precision=highest)
    empty = jnp.zeros((1, HEADS, DH, DH), jnp.float32)
    prefix_states = jnp.concatenate([empty, jnp.cumsum(local_states, axis=0)[:-1]], axis=0)
    attention, inverse_rms = lax.map(forward_block, (query_blocks, key_blocks, value_blocks, prefix_states))
    normed = (attention * inverse_rms * gain_heads).astype(jnp.bfloat16).reshape(TOKENS, D)
    mixed = jnp.dot(normed, out_weight, preferred_element_type=jnp.float32).astype(jnp.bfloat16)
    grad_normed = jnp.dot(grad_output, out_weight.T, preferred_element_type=jnp.float32).reshape(blocks, TOK_DEV, HEADS, DH)
    grad_gain = lax.optimization_barrier(jnp.sum(grad_normed * attention * inverse_rms, axis=(0, 1))).reshape(D)
    gained = grad_normed * gain_heads
    cubed = inverse_rms * inverse_rms * inverse_rms
    grad_attention = inverse_rms * gained - attention * cubed * lax.optimization_barrier(jnp.mean(gained * attention, axis=-1, keepdims=True))
    state_terms = jnp.einsum('bthd,bthe->bhde', query_blocks.astype(jnp.float32), grad_attention, precision=highest)
    later_sums = jnp.cumsum(state_terms[::-1], axis=0)[::-1]
    suffix_states = jnp.concatenate([later_sums[1:], empty], axis=0)
    grad_queries, grad_keys, grad_values = lax.map(backward_block, (query_blocks, key_blocks, value_blocks, prefix_states, suffix_states, grad_attention))
    return (mixed, grad_queries.reshape(TOKENS, D), grad_keys.reshape(TOKENS, D), grad_values.reshape(TOKENS, D), grad_gain)
```

```python
import functools

import jax
import jax.numpy as jnp
from jax import lax
from jax.experimental import pallas as pl
from jax.experimental.pallas import tpu as pltpu
from jax.sharding import PartitionSpec as P

DH = 128
QUAD = 4
EXTRA = 16
EPSILON = 1e-05
wide = jnp.float32
low = jnp.bfloat16
VMEM = pl.BlockSpec(memory_space=pltpu.VMEM)
SMEM = pl.BlockSpec(memory_space=pltpu.SMEM)


def dot(a, b, over):
    return lax.dot_general(a, b, (((over[0],), (over[1],)), ((), ())), preferred_element_type=wide)


def shaped(shape, dtype):
    return jax.ShapeDtypeStruct(shape, dtype)


def call(body, outs, ins, flops, moved):
    return pl.pallas_call(
        body,
        out_shape=outs,
        in_specs=ins,
        out_specs=[VMEM] * len(outs),
        cost_estimate=pl.CostEstimate(flops=flops, bytes_accessed=moved, transcendentals=0),
        compiler_params=pltpu.CompilerParams(vmem_limit_bytes=32 * 2**20),
    )


def head_slices(place, per_quarter):
    for j in range(QUAD):
        for i in range(per_quarter):
            start = ((place ^ j) * per_quarter + i) * DH
            yield j, i, pl.ds(pl.multiple_of(start, DH), DH)


def state_kernel(per_quarter, place_ref, key_ref, value_ref, *out_refs):
    for j, i, head in head_slices(place_ref[0], per_quarter):
        state = dot(key_ref[:, head], value_ref[:, head], (0, 0))
        out_refs[j][i * DH : (i + 1) * DH, :] = state.astype(low)


def causal(tokens):
    rows = lax.broadcasted_iota(jnp.int32, (tokens, tokens), 0)
    columns = lax.broadcasted_iota(jnp.int32, (tokens, tokens), 1)
    return rows >= columns


def local_kernel(heads, query_ref, key_ref, value_ref, score_ref, local_ref):
    keep = causal(query_ref.shape[0])
    for h in range(heads):
        head = slice(h * DH, (h + 1) * DH)
        scores = dot(query_ref[:, head], key_ref[:, head], (1, 1))
        scores = jnp.where(keep, scores, 0.0).astype(low)
        score_ref[h] = scores
        local_ref[:, head] = dot(scores, value_ref[:, head], (1, 0))


def norm_kernel(
    per_quarter, place_ref, query_ref, local_ref, grad_ref, gain_ref, p0, p1, p2, p3,
    normed_ref, low_ref, *out_refs
):
    prefix = (p0, p1, p2, p3)
    for j, i, head in head_slices(place_ref[0], per_quarter):
        rows = slice(i * DH, (i + 1) * DH)
        query = query_ref[:, head]
        attention = local_ref[:, head] + dot(query, prefix[j][rows, :], (1, 0))
        inverse = lax.rsqrt(jnp.mean(attention * attention, axis=-1, keepdims=True) + EPSILON)
        scaled = attention * inverse
        gain = gain_ref[:, head]
        normed_ref[:, head] = (scaled * gain).astype(low)
        grad = grad_ref[:, head]
        gain_term = jnp.sum(grad * scaled, axis=0, keepdims=True)
        gained = grad * gain
        inner = jnp.mean(gained * scaled, axis=-1, keepdims=True)
        grad_low = (inverse * (gained - scaled * inner)).astype(low)
        low_ref[:, head] = grad_low
        out_refs[j][rows, :] = dot(query, grad_low, (0, 0)).astype(low)
        upper = gain_term.astype(low)
        base = per_quarter * DH
        if i == 0:
            out_refs[j][base:, :] = jnp.zeros((EXTRA, DH), low)
        out_refs[j][base + 2 * i : base + 2 * i + 1, :] = upper
        out_refs[j][base + 2 * i + 1 : base + 2 * i + 2, :] = (
            gain_term - upper.astype(wide)
        ).astype(low)


def grad_kernel(
    per_quarter, place_ref, query_ref, key_ref, value_ref, low_ref, score_ref, p0, p1, p2, p3,
    grad_query_ref, grad_key_ref, grad_value_ref
):
    prefix = (p0, p1, p2, p3)
    keep = causal(query_ref.shape[0])
    for j, i, head in head_slices(place_ref[0], per_quarter):
        rows = slice(i * DH, (i + 1) * DH)
        grad_low = low_ref[:, head]
        raw = dot(grad_low, value_ref[:, head], (1, 1))
        grad_scores = jnp.where(keep, raw, 0.0).astype(low)
        grad_query = dot(grad_scores, key_ref[:, head], (1, 0))
        grad_query = grad_query + dot(grad_low, prefix[j][rows, :], (1, 1))
        grad_query_ref[:, head] = grad_query.astype(low)
        grad_key_ref[:, head] = dot(grad_scores, query_ref[:, head], (0, 0))
        scores = score_ref[(place_ref[0] ^ j) * per_quarter + i]
        grad_value_ref[:, head] = dot(scores, grad_low, (0, 0))


def finish_kernel(
    per_quarter, place_ref, key_ref, value_ref, local_key_ref, local_value_ref, own_ref, other_ref,
    s0, s1, s2, s3, grad_key_ref, grad_value_ref, mixed_ref
):
    suffix = (s0, s1, s2, s3)
    for j, i, head in head_slices(place_ref[0], per_quarter):
        rows = slice(i * DH, (i + 1) * DH)
        state = suffix[j][rows, :]
        grad_key = local_key_ref[:, head] + dot(value_ref[:, head], state, (1, 1))
        grad_key_ref[:, head] = grad_key.astype(low)
        grad_value = local_value_ref[:, head] + dot(key_ref[:, head], state, (1, 0))
        grad_value_ref[:, head] = grad_value.astype(low)
    mixed_ref[...] = (own_ref[...] + other_ref[...].astype(wide)).astype(low)


def back_kernel(side_ref, own_ref, other_ref, weight_ref, out_ref):
    width = own_ref.shape[1]
    own = pl.ds(pl.multiple_of(side_ref[0] * width, DH), width)
    other = pl.ds(pl.multiple_of((1 - side_ref[0]) * width, DH), width)
    total = dot(own_ref[...], weight_ref[:, own], (1, 1))
    out_ref[...] = total + dot(other_ref[...], weight_ref[:, other], (1, 1))


def project_kernel(normed_ref, weight_ref, out_ref):
    out_ref[...] = dot(normed_ref[...], weight_ref[...], (1, 0)).astype(out_ref.dtype)


def project(side, normed, weight, dtype):
    tokens, rows = normed.shape
    half = weight.shape[1] // 2
    block = half // 4

    def body(side_ref, normed_ref, weight_ref, out_ref):
        project_kernel(normed_ref, weight_ref, out_ref)

    return pl.pallas_call(
        body,
        out_shape=shaped((tokens, half), dtype),
        grid_spec=pltpu.PrefetchScalarGridSpec(
            num_scalar_prefetch=1,
            grid=(4,),
            in_specs=[
                pl.BlockSpec((tokens, rows), lambda c, s: (0, 0)),
                pl.BlockSpec((rows, block), lambda c, s: (0, s[0] * 4 + c)),
            ],
            out_specs=pl.BlockSpec((tokens, block), lambda c, s: (0, c)),
        ),
        cost_estimate=pl.CostEstimate(
            flops=2 * tokens * rows * half, bytes_accessed=2 * rows * half, transcendentals=0
        ),
    )(side, normed, weight)


def back_project(side, own, other, weight):
    tokens, width = own.shape
    rows = weight.shape[0]
    block = rows // 4
    return pl.pallas_call(
        back_kernel,
        out_shape=shaped((tokens, rows), wide),
        grid_spec=pltpu.PrefetchScalarGridSpec(
            num_scalar_prefetch=1,
            grid=(4,),
            in_specs=[
                pl.BlockSpec((tokens, width), lambda c, s: (0, 0)),
                pl.BlockSpec((tokens, width), lambda c, s: (0, 0)),
                pl.BlockSpec((block, 2 * width), lambda c, s: (c, 0)),
            ],
            out_specs=pl.BlockSpec((tokens, block), lambda c, s: (0, c)),
        ),
        cost_estimate=pl.CostEstimate(
            flops=4 * tokens * rows * width, bytes_accessed=4 * rows * width, transcendentals=0
        ),
    )(side, own, other, weight)


def swap(array, flip):
    count = lax.axis_size("seq")
    return lax.ppermute(array, "seq", [(i, i ^ flip) for i in range(count)])


def trade(array):
    return lax.ppermute(array, "tensor", [(0, 1), (1, 0)])


def scan(parts, backward, rows, gains):
    count = lax.axis_size("seq")
    place = lax.axis_index("seq")
    quarter = place % QUAD
    blocks = [parts[0]] + [swap(parts[j], j) for j in range(1, QUAD)]
    states = [block[:rows].astype(wide) for block in blocks]
    total = states[0] + states[1] + states[2] + states[3]
    outside = jnp.zeros_like(total)
    gain = None
    if gains:
        gain = sum(gain_of(block, rows, gains) for block in blocks)
    step = QUAD
    while step < count:
        got = swap(pack(total, gain), step)
        state = got[:rows].astype(wide)
        beyond = ((place & step) == 0) if backward else ((place & step) != 0)
        outside = outside + jnp.where(beyond, state, 0.0)
        total = total + state
        if gains:
            gain = gain + gain_of(got, rows, gains)
        step *= 2
    results = []
    for j in range(QUAD):
        target = quarter ^ j
        result = outside
        for i in range(QUAD):
            source = quarter ^ i
            counts = (source > target) if backward else (source < target)
            result = result + jnp.where(counts, states[i], 0.0)
        results.append(pack(result, gain))
    back = [results[0]] + [swap(results[j], j) for j in range(1, QUAD)]
    return back, gain


def gain_of(block, rows, gains):
    pairs = block[rows : rows + 2 * gains].astype(wide).reshape(gains, 2, DH)
    return pairs[:, 0] + pairs[:, 1]


def pack(state, gain):
    if gain is None:
        return state.astype(low)
    upper = gain.astype(low)
    lower = (gain - upper.astype(wide)).astype(low)
    pairs = jnp.stack([upper, lower], axis=1).reshape(-1, DH)
    spare = jnp.zeros((EXTRA - pairs.shape[0], DH), low)
    return jnp.concatenate([state.astype(low), pairs, spare], axis=0)


def on_device(queries, key_vectors, values, out_weight, norm_gain, grad_output):
    tokens, width = queries.shape
    heads = width // DH
    per_quarter = heads // QUAD
    rows = per_quarter * DH
    place = lax.axis_index("seq")
    quarter = (place % QUAD).astype(jnp.int32)
    order = quarter.reshape(1)
    side = lax.axis_index("tensor").astype(jnp.int32).reshape(1)
    gain_row = norm_gain.reshape(1, width)
    whole = shaped((tokens, width), wide)
    whole_low = shaped((tokens, width), low)
    small = 2 * tokens * width * DH

    other_grad = trade(grad_output)
    parts = call(
        functools.partial(state_kernel, per_quarter),
        [shaped((rows, DH), low)] * QUAD,
        [SMEM, VMEM, VMEM],
        small,
        4 * tokens * width,
    )(order, key_vectors, values)
    prefix, _ = scan(parts, False, rows, 0)

    scores, local = call(
        functools.partial(local_kernel, heads),
        [shaped((heads, tokens, tokens), low), whole],
        [VMEM] * 3,
        4 * heads * tokens * tokens * DH,
        12 * tokens * width,
    )(queries, key_vectors, values)
    grad_normed = back_project(side, grad_output, other_grad, out_weight)

    normed, grad_low, *terms = call(
        functools.partial(norm_kernel, per_quarter),
        [whole_low, whole_low] + [shaped((rows + EXTRA, DH), low)] * QUAD,
        [SMEM] + [VMEM] * 8,
        2 * small,
        14 * tokens * width,
    )(order, queries, local, grad_normed, gain_row, *prefix)
    suffix, _ = scan(terms, True, rows, per_quarter)

    sent = project(1 - side, normed, out_weight, low)
    other_part = trade(sent)
    own_part = project(side, normed, out_weight, wide)
    grad_queries, local_keys, local_values = call(
        functools.partial(grad_kernel, per_quarter),
        [whole_low, whole, whole],
        [SMEM] + [VMEM] * 9,
        8 * heads * tokens * tokens * DH + small,
        20 * tokens * width,
    )(order, queries, key_vectors, values, grad_low, scores, *prefix)

    grad_keys, grad_values, mixed = call(
        functools.partial(finish_kernel, per_quarter),
        [whole_low, whole_low, whole_low],
        [SMEM] + [VMEM] * 10,
        2 * small,
        20 * tokens * width,
    )(order, key_vectors, values, local_keys, local_values, own_part, other_part, *suffix)

    gains = jnp.stack([gain_of(part, rows, per_quarter) for part in suffix])
    natural = jnp.zeros_like(gains)
    for t in range(QUAD):
        for j in range(QUAD):
            natural = natural.at[t].add(jnp.where((quarter ^ j) == t, gains[j], 0.0))
    return mixed, grad_queries, grad_keys, grad_values, natural.reshape(width)


def solution(mesh):
    placed = (
        P(("parts", "seq"), "tensor"),
        P(("parts", "seq"), "tensor"),
        P(("parts", "seq"), "tensor"),
        P("tensor", None),
        P("tensor"),
        P(("parts", "seq"), "tensor"),
    )
    return jax.shard_map(
        on_device,
        mesh=mesh,
        in_specs=placed,
        out_specs=(
            P(("parts", "seq"), "tensor"),
            P(("parts", "seq"), "tensor"),
            P(("parts", "seq"), "tensor"),
            P(("parts", "seq"), "tensor"),
            P(("parts", "tensor")),
        ),
        check_vma=False,
    )
```

```python
import functools

import jax
import jax.numpy as jnp
from jax import lax
from jax.experimental import pallas as pl
from jax.experimental.pallas import tpu as pltpu
from jax.sharding import PartitionSpec as P

DH = 128
QUAD = 4
EXTRA = 16
CHUNK = 512
COST = 1000
EPSILON = 1e-05
wide = jnp.float32
low = jnp.bfloat16
VMEM = pl.BlockSpec(memory_space=pltpu.VMEM)
SMEM = pl.BlockSpec(memory_space=pltpu.SMEM)
HBM = pl.BlockSpec(memory_space=pltpu.HBM)
FREE = pl.BlockSpec(memory_space=pltpu.VMEM)


def dot(a, b, over):
    return lax.dot_general(a, b, (((over[0],), (over[1],)), ((), ())), preferred_element_type=wide)


def shaped(shape, dtype):
    return jax.ShapeDtypeStruct(shape, dtype)


def call(body, outs, ins, out_specs=None, scratch=(), room=6):
    out_specs = out_specs or [VMEM] * len(outs)
    placed = [
        pltpu.VMEM(out.shape, out.dtype) if spec is VMEM else out for out, spec in zip(outs, out_specs)
    ]
    kernel = pl.pallas_call(
        body,
        out_shape=placed,
        in_specs=[VMEM if spec is FREE else spec for spec in ins],
        out_specs=[VMEM if spec is FREE else spec for spec in out_specs],
        scratch_shapes=list(scratch),
        cost_estimate=pl.CostEstimate(flops=COST, bytes_accessed=COST, transcendentals=0),
        compiler_params=pltpu.CompilerParams(vmem_limit_bytes=room * 2**20),
    )

    def pinned(*operands):
        spaces = {id(VMEM): pltpu.VMEM, id(HBM): pltpu.HBM}
        fixed = [
            pltpu.with_memory_space_constraint(operand, spaces[id(spec)]) if id(spec) in spaces else operand
            for operand, spec in zip(operands, ins, strict=True)
        ]
        return kernel(*fixed)

    return pinned


def head_slices(place, per_quarter):
    for j in range(QUAD):
        for i in range(per_quarter):
            start = ((place ^ j) * per_quarter + i) * DH
            yield j, i, pl.ds(pl.multiple_of(start, DH), DH)


def state_kernel(per_quarter, place_ref, key_hbm, value_hbm, *rest):
    out_refs, key_ref, value_ref, sems = rest[:QUAD], rest[QUAD], rest[QUAD + 1], rest[QUAD + 2]
    copies = [
        pltpu.make_async_copy(key_hbm, key_ref, sems.at[0]),
        pltpu.make_async_copy(value_hbm, value_ref, sems.at[1]),
    ]
    for copy in copies:
        copy.start()
    for copy in copies:
        copy.wait()
    for j, i, head in head_slices(place_ref[0], per_quarter):
        state = dot(key_ref[:, head], value_ref[:, head], (0, 0))
        out_refs[j][i * DH : (i + 1) * DH, :] = state.astype(low)


def causal(tokens):
    rows = lax.broadcasted_iota(jnp.int32, (tokens, tokens), 0)
    columns = lax.broadcasted_iota(jnp.int32, (tokens, tokens), 1)
    return rows >= columns


def local_kernel(heads, query_hbm, key_ref, value_ref, local_ref, query_ref, sems):
    copy = pltpu.make_async_copy(query_hbm, query_ref, sems.at[0])
    copy.start()
    keep = causal(query_ref.shape[0])
    copy.wait()
    for h in range(heads):
        head = slice(h * DH, (h + 1) * DH)
        scores = dot(query_ref[:, head], key_ref[:, head], (1, 1))
        scores = jnp.where(keep, scores, 0.0).astype(low)
        local_ref[:, head] = dot(scores, value_ref[:, head], (1, 0))


def norm_kernel(
    per_quarter, place_ref, query_ref, local_ref, grad_ref, gain_ref, p0, p1, p2, p3,
    normed_ref, low_ref, *out_refs
):
    prefix = (p0, p1, p2, p3)
    for j, i, head in head_slices(place_ref[0], per_quarter):
        rows = slice(i * DH, (i + 1) * DH)
        query = query_ref[:, head]
        attention = local_ref[:, head] + dot(query, prefix[j][rows, :], (1, 0))
        inverse = lax.rsqrt(jnp.mean(attention * attention, axis=-1, keepdims=True) + EPSILON)
        scaled = attention * inverse
        gain = gain_ref[:, head]
        normed_ref[:, head] = (scaled * gain).astype(low)
        grad = grad_ref[:, head]
        gain_term = jnp.sum(grad * scaled, axis=0, keepdims=True)
        gained = grad * gain
        inner = jnp.mean(gained * scaled, axis=-1, keepdims=True)
        grad_low = (inverse * (gained - scaled * inner)).astype(low)
        low_ref[:, head] = grad_low
        out_refs[j][rows, :] = dot(query, grad_low, (0, 0)).astype(low)
        if i == 0:
            out_refs[j][per_quarter * DH :, :] = jnp.zeros((EXTRA, DH), low)
        put_pair(out_refs[j], per_quarter, i, gain_term)


def grad_kernel(
    per_quarter, place_ref, query_ref, key_ref, value_ref, low_ref, p0, p1, p2, p3,
    grad_query_ref, grad_key_ref, grad_value_ref
):
    prefix = (p0, p1, p2, p3)
    keep = causal(query_ref.shape[0])
    for j, i, head in head_slices(place_ref[0], per_quarter):
        rows = slice(i * DH, (i + 1) * DH)
        grad_low = low_ref[:, head]
        raw = dot(grad_low, value_ref[:, head], (1, 1))
        grad_scores = jnp.where(keep, raw, 0.0).astype(low)
        grad_query = dot(grad_scores, key_ref[:, head], (1, 0))
        grad_query = grad_query + dot(grad_low, prefix[j][rows, :], (1, 1))
        grad_query_ref[:, head] = grad_query.astype(low)
        grad_key_ref[:, head] = dot(grad_scores, query_ref[:, head], (0, 0)).astype(low)
        scores = dot(query_ref[:, head], key_ref[:, head], (1, 1))
        scores = jnp.where(keep, scores, 0.0).astype(low)
        grad_value_ref[:, head] = dot(scores, grad_low, (0, 0)).astype(low)


def finish_kernel(
    per_quarter, place_ref, key_ref, value_ref, local_key_ref, local_value_ref,
    s0, s1, s2, s3, grad_key_hbm, grad_value_hbm, gain_ref, key_out, value_out, sems
):
    suffix = (s0, s1, s2, s3)
    copies = []
    for j, i, head in head_slices(place_ref[0], per_quarter):
        rows = slice(i * DH, (i + 1) * DH)
        slot = j * per_quarter + i
        state = suffix[j][rows, :]
        grad_key = local_key_ref[:, head].astype(wide) + dot(value_ref[:, head], state, (1, 1))
        key_out[:, head] = grad_key.astype(low)
        grad_value = local_value_ref[:, head].astype(wide) + dot(key_ref[:, head], state, (1, 0))
        value_out[:, head] = grad_value.astype(low)
        copies.append(pltpu.make_async_copy(key_out.at[:, head], grad_key_hbm.at[:, head], sems.at[0, slot]))
        copies.append(pltpu.make_async_copy(value_out.at[:, head], grad_value_hbm.at[:, head], sems.at[1, slot]))
        for copy in copies[-2:]:
            copy.start()
        gain_ref[:, head] = pair_sum(suffix[j], per_quarter, i)
    for copy in copies:
        copy.wait()


def pair_sum(ref, per_quarter, i):
    base = per_quarter * DH + 2 * i
    return ref[base : base + 1, :].astype(wide) + ref[base + 1 : base + 2, :].astype(wide)


def put_pair(ref, per_quarter, i, gain):
    base = per_quarter * DH + 2 * i
    upper = gain.astype(low)
    ref[base : base + 1, :] = upper
    ref[base + 1 : base + 2, :] = (gain - upper.astype(wide)).astype(low)


def back_kernel(side_ref, own_hbm, other_ref, weight_hbm, out_ref, own_ref, weight_ref, own_sem, sems):
    width = own_ref.shape[1]
    own = pl.ds(pl.multiple_of(side_ref[0] * width, DH), width)
    other = pl.ds(pl.multiple_of((1 - side_ref[0]) * width, DH), width)
    own_copy = pltpu.make_async_copy(own_hbm, own_ref, own_sem.at[0])
    own_copy.start()
    chunks = [slice(start, start + CHUNK) for start in range(0, weight_ref.shape[0], CHUNK)]
    copies = [
        pltpu.make_async_copy(weight_hbm.at[rows, :], weight_ref.at[rows, :], sems.at[c])
        for c, rows in enumerate(chunks)
    ]
    for copy in copies:
        copy.start()
    own_copy.wait()
    for copy, rows in zip(copies, chunks):
        copy.wait()
        total = dot(own_ref[...], weight_ref[rows, own], (1, 1))
        out_ref[:, rows] = total + dot(other_ref[...], weight_ref[rows, other], (1, 1))


def column_chunks(start, weight_hbm, weight_ref, sems):
    copies = []
    for c, column in enumerate(range(0, weight_ref.shape[1], CHUNK)):
        source = pl.ds(pl.multiple_of(start + column, DH), CHUNK)
        columns = slice(column, column + CHUNK)
        copy = pltpu.make_async_copy(weight_hbm.at[:, source], weight_ref.at[:, columns], sems.at[c])
        copy.start()
        copies.append((copy, columns))
    return copies


def send_kernel(side_ref, normed_ref, weight_hbm, out_ref, weight_ref, sems):
    start = (1 - side_ref[0]) * out_ref.shape[1]
    for copy, columns in column_chunks(start, weight_hbm, weight_ref, sems):
        copy.wait()
        out_ref[:, columns] = dot(normed_ref[...], weight_ref[:, columns], (1, 0)).astype(low)


def mixed_kernel(side_ref, normed_ref, weight_hbm, other_ref, out_ref, weight_ref, sems):
    start = side_ref[0] * out_ref.shape[1]
    for copy, columns in column_chunks(start, weight_hbm, weight_ref, sems):
        copy.wait()
        total = dot(normed_ref[...], weight_ref[:, columns], (1, 0))
        out_ref[:, columns] = (total + other_ref[:, columns].astype(wide)).astype(low)


def first_kernel(gains, keep, b0, b1, b2, b3, send_ref, *refs):
    rows = send_ref.shape[0] - (EXTRA if gains else 0)
    blocks = (b0, b1, b2, b3)
    total = sum(block[:rows, :].astype(wide) for block in blocks)
    send_ref[:rows, :] = total.astype(low)
    gain_refs = refs[keep:]
    if keep:
        refs[0][...] = total
    spread_gain(gains, send_ref, gain_refs, blocks, None)


def spread_gain(gains, send_ref, gain_refs, blocks, earlier):
    if not gains:
        return
    send_ref[gains * DH :, :] = jnp.zeros((EXTRA, DH), low)
    for i in range(gains):
        gain = sum(pair_sum(block, gains, i) for block in blocks)
        if earlier is not None:
            gain = gain + earlier[i : i + 1, :]
        gain_refs[0][i : i + 1, :] = gain
        put_pair(send_ref, gains, i, gain)


def step_kernel(gains, past, beyond_ref, total_ref, got_ref, *refs):
    refs = list(refs)
    outside_ref = refs.pop(0) if past else None
    earlier = refs.pop(0) if gains else None
    total_out, outside_out, send_ref = refs[:3]
    rows = total_ref.shape[0]
    state = got_ref[:rows, :].astype(wide)
    outside = jnp.where(beyond_ref[0] != 0, state, 0.0)
    outside_out[...] = outside + outside_ref[...] if past else outside
    total = total_ref[...] + state
    total_out[...] = total
    send_ref[:rows, :] = total.astype(low)
    spread_gain(gains, send_ref, refs[3:], (got_ref,), earlier)


def last_kernel(gains, past, backward, place_ref, beyond_ref, b0, b1, b2, b3, got_ref, *refs):
    refs = list(refs)
    outside_ref = refs.pop(0) if past else None
    earlier = refs.pop(0) if gains else None
    blocks = (b0, b1, b2, b3)
    rows = got_ref.shape[0] - (EXTRA if gains else 0)
    quarter = place_ref[0]
    outside = jnp.where(beyond_ref[0] != 0, got_ref[:rows, :].astype(wide), 0.0)
    if past:
        outside = outside + outside_ref[...]
    states = [block[:rows, :].astype(wide) for block in blocks]
    for j in range(QUAD):
        result = outside
        for i in range(QUAD):
            if i == j:
                continue
            source, target = quarter ^ i, quarter ^ j
            counts = (source > target) if backward else (source < target)
            result = result + jnp.where(counts, states[i], 0.0)
        refs[j][:rows, :] = result.astype(low)
        if gains:
            refs[j][rows:, :] = jnp.zeros((EXTRA, DH), low)
    for i in range(gains):
        gain = earlier[i : i + 1, :] + pair_sum(got_ref, gains, i)
        for j in range(QUAD):
            put_pair(refs[j], gains, i, gain)


def swap(array, flip):
    count = lax.axis_size("seq")
    return lax.ppermute(array, "seq", [(i, i ^ flip) for i in range(count)])


def trade(array):
    return lax.ppermute(array, "tensor", [(0, 1), (1, 0)])


def scan(order, parts, backward, rows, gains, before_first, before_last):
    count = lax.axis_size("seq")
    place = lax.axis_index("seq")
    blocks = [parts[0]] + [swap(parts[j], j) for j in range(1, QUAD)]
    blocks, before_first = lax.optimization_barrier((blocks, before_first))
    total_shape = [shaped((rows, DH), wide)]
    part_shape = [shaped(parts[0].shape, low)]
    gain_shape = [shaped((gains, DH), wide)] if gains else []
    keep = int(count > 2 * QUAD)
    send, *rest = call(
        functools.partial(first_kernel, gains, keep),
        part_shape + total_shape * keep + gain_shape,
        [VMEM] * QUAD,
    )(*blocks)
    total, gain = rest[:keep], rest[keep:]
    outside = []
    step = QUAD
    while True:
        got = swap(send, step)
        bit = (place & step) != 0
        beyond = (jnp.logical_not(bit) if backward else bit).astype(jnp.int32).reshape(1)
        if 2 * step >= count:
            break
        new_total, new_outside, send, *gain = call(
            functools.partial(step_kernel, gains, len(outside)),
            total_shape * 2 + part_shape + gain_shape,
            [SMEM] + [VMEM] * (2 + len(outside) + len(gain)),
        )(beyond, *total, got, *outside, *gain)
        total, outside = [new_total], [new_outside]
        step *= 2
    got, before_last = lax.optimization_barrier((got, before_last))
    results = call(
        functools.partial(last_kernel, gains, len(outside), backward),
        part_shape * QUAD,
        [SMEM, SMEM] + [VMEM] * (QUAD + 1 + len(outside) + len(gain)),
    )(order, beyond, *blocks, got, *outside, *gain)
    back = [results[0]] + [swap(results[j], j) for j in range(1, QUAD)]
    return back, before_first, before_last


def on_device(queries, key_vectors, values, out_weight, norm_gain, grad_output):
    tokens, width = queries.shape
    model = out_weight.shape[1]
    heads = width // DH
    per_quarter = heads // QUAD
    rows = per_quarter * DH
    place = lax.axis_index("seq")
    order = (place & (QUAD - 1)).astype(jnp.int32).reshape(1)
    side = lax.axis_index("tensor").astype(jnp.int32).reshape(1)
    gain_row = norm_gain.reshape(1, width)
    whole = shaped((tokens, width), wide)
    whole_low = shaped((tokens, width), low)
    head_sems = pltpu.SemaphoreType.DMA((2, heads))
    half = model // 2
    weight_half = [pltpu.VMEM((width, half), low), pltpu.SemaphoreType.DMA((half // CHUNK,))]
    weight_whole = [pltpu.VMEM((width, model), low), pltpu.SemaphoreType.DMA((1,)), pltpu.SemaphoreType.DMA((width // CHUNK,))]

    other_grad = trade(grad_output)
    *parts, key_near, value_near = call(
        functools.partial(state_kernel, per_quarter),
        [shaped((rows, DH), low)] * QUAD + [whole_low, whole_low],
        [SMEM, HBM, HBM],
        scratch=[pltpu.SemaphoreType.DMA((2,))],
    )(order, key_vectors, values)
    local, query_near = call(
        functools.partial(local_kernel, heads),
        [whole, whole_low],
        [HBM, VMEM, VMEM],
        scratch=[pltpu.SemaphoreType.DMA((1,))],
    )(queries, key_near, value_near)
    (grad_normed,) = call(
        back_kernel,
        [whole],
        [SMEM, HBM, VMEM, HBM],
        scratch=[pltpu.VMEM((tokens, half), low)] + weight_whole,
        room=12,
    )(side, grad_output, other_grad, out_weight)
    prefix, grad_normed, local = scan(order, parts, False, rows, 0, grad_normed, local)

    normed, grad_low, *terms = call(
        functools.partial(norm_kernel, per_quarter),
        [whole_low, whole_low] + [shaped((rows + EXTRA, DH), low)] * QUAD,
        [SMEM, VMEM, VMEM, VMEM, FREE] + [VMEM] * 4,
    )(order, query_near, local, grad_normed, gain_row, *prefix)

    (sent,) = call(
        send_kernel, [whole_low], [SMEM, VMEM, HBM], out_specs=[FREE], scratch=weight_half, room=8
    )(
        side, normed, out_weight
    )
    grad_queries, local_keys, local_values = call(
        functools.partial(grad_kernel, per_quarter),
        [whole_low, whole_low, whole_low],
        [SMEM] + [VMEM] * 8,
        out_specs=[FREE, VMEM, VMEM],
    )(order, query_near, key_near, value_near, grad_low, *prefix)
    suffix, local_keys, sent = scan(order, terms, True, rows, per_quarter, local_keys, sent)
    other_part = trade(sent)
    (mixed,) = call(
        mixed_kernel,
        [whole_low],
        [SMEM, VMEM, HBM, VMEM],
        out_specs=[FREE],
        scratch=weight_half,
        room=8,
    )(side, normed, out_weight, other_part)
    mixed, local_keys = lax.optimization_barrier((mixed, local_keys))

    grad_keys, grad_values, grad_gain = call(
        functools.partial(finish_kernel, per_quarter),
        [whole_low, whole_low, shaped((1, width), wide)],
        [SMEM] + [VMEM] * 8,
        out_specs=[HBM, HBM, FREE],
        scratch=[pltpu.VMEM((tokens, width), low), pltpu.VMEM((tokens, width), low), head_sems],
    )(order, key_near, value_near, local_keys, local_values, *suffix)
    return mixed, grad_queries, grad_keys, grad_values, grad_gain.reshape(width)


def solution(mesh):
    placed = (
        P(("parts", "seq"), "tensor"),
        P(("parts", "seq"), "tensor"),
        P(("parts", "seq"), "tensor"),
        P("tensor", None),
        P("tensor"),
        P(("parts", "seq"), "tensor"),
    )
    return jax.shard_map(
        on_device,
        mesh=mesh,
        in_specs=placed,
        out_specs=(
            P(("parts", "seq"), "tensor"),
            P(("parts", "seq"), "tensor"),
            P(("parts", "seq"), "tensor"),
            P(("parts", "seq"), "tensor"),
            P(("parts", "tensor")),
        ),
        check_vma=False,
    )
```

```python
import functools

import jax
import jax.numpy as jnp
from jax import lax
from jax.experimental import pallas as pl
from jax.experimental.pallas import tpu as pltpu
from jax.sharding import PartitionSpec as P

DH = 128
QUAD = 4
EXTRA = 16
CHUNK = 512
COST = 1000
FINISH = ((0, 1), (2, 3))
EPSILON = 1e-05
wide = jnp.float32
low = jnp.bfloat16
VMEM = pl.BlockSpec(memory_space=pltpu.VMEM)
SMEM = pl.BlockSpec(memory_space=pltpu.SMEM)
HBM = pl.BlockSpec(memory_space=pltpu.HBM)
FREE = pl.BlockSpec(memory_space=pltpu.VMEM)


def dot(a, b, over):
    return lax.dot_general(a, b, (((over[0],), (over[1],)), ((), ())), preferred_element_type=wide)


def shaped(shape, dtype):
    return jax.ShapeDtypeStruct(shape, dtype)


def call(body, outs, ins, out_specs=None, scratch=(), room=6, aliases=None):
    out_specs = out_specs or [VMEM] * len(outs)
    placed = [
        pltpu.VMEM(out.shape, out.dtype) if spec is VMEM else out for out, spec in zip(outs, out_specs)
    ]
    kernel = pl.pallas_call(
        body,
        out_shape=placed,
        in_specs=[VMEM if spec is FREE else spec for spec in ins],
        out_specs=[VMEM if spec is FREE else spec for spec in out_specs],
        scratch_shapes=list(scratch),
        input_output_aliases=aliases or {},
        cost_estimate=pl.CostEstimate(flops=COST, bytes_accessed=COST, transcendentals=0),
        compiler_params=pltpu.CompilerParams(vmem_limit_bytes=room * 2**20),
    )

    def pinned(*operands):
        spaces = {id(VMEM): pltpu.VMEM, id(HBM): pltpu.HBM}
        fixed = [
            pltpu.with_memory_space_constraint(operand, spaces[id(spec)]) if id(spec) in spaces else operand
            for operand, spec in zip(operands, ins, strict=True)
        ]
        return kernel(*fixed)

    return pinned


def head_slices(place, per_quarter, quarters=range(QUAD)):
    for j in quarters:
        for i in range(per_quarter):
            start = (((place & (QUAD - 1)) ^ j) * per_quarter + i) * DH
            yield j, i, pl.ds(pl.multiple_of(start, DH), DH)


def state_kernel(per_quarter, place_ref, key_hbm, value_hbm, *rest):
    out_refs, key_ref, value_ref, sems = rest[:QUAD], rest[QUAD], rest[QUAD + 1], rest[QUAD + 2]
    copies = [
        pltpu.make_async_copy(key_hbm, key_ref, sems.at[0]),
        pltpu.make_async_copy(value_hbm, value_ref, sems.at[1]),
    ]
    for copy in copies:
        copy.start()
    for copy in copies:
        copy.wait()
    for j, i, head in head_slices(place_ref[0], per_quarter):
        state = dot(key_ref[:, head], value_ref[:, head], (0, 0))
        out_refs[j][i * DH : (i + 1) * DH, :] = state.astype(low)


def causal(tokens):
    rows = lax.broadcasted_iota(jnp.int32, (tokens, tokens), 0)
    columns = lax.broadcasted_iota(jnp.int32, (tokens, tokens), 1)
    return rows >= columns


def local_kernel(heads, query_hbm, key_ref, value_ref, local_ref, query_ref, score_ref, sems):
    copy = pltpu.make_async_copy(query_hbm, query_ref, sems.at[0])
    copy.start()
    keep = causal(query_ref.shape[0])
    copy.wait()
    for h in range(heads):
        head = slice(h * DH, (h + 1) * DH)
        scores = dot(query_ref[:, head], key_ref[:, head], (1, 1))
        scores = jnp.where(keep, scores, 0.0).astype(low)
        score_ref[h] = scores
        local_ref[:, head] = dot(scores, value_ref[:, head], (1, 0))


def norm_kernel(
    per_quarter, j, place_ref, query_ref, local_ref, grad_ref, gain_ref, prefix_ref,
    normed_ref, low_ref, out_ref
):
    for _, i, head in head_slices(place_ref[0], per_quarter, (j,)):
        rows = slice(i * DH, (i + 1) * DH)
        query = query_ref[:, head]
        attention = local_ref[:, head] + dot(query, prefix_ref[rows, :], (1, 0))
        inverse = lax.rsqrt(jnp.mean(attention * attention, axis=-1, keepdims=True) + EPSILON)
        scaled = attention * inverse
        gain = gain_ref[:, head]
        normed_ref[:, rows] = (scaled * gain).astype(low)
        grad = grad_ref[:, head]
        gain_term = jnp.sum(grad * scaled, axis=0, keepdims=True)
        gained = grad * gain
        inner = jnp.mean(gained * scaled, axis=-1, keepdims=True)
        grad_low = (inverse * (gained - scaled * inner)).astype(low)
        low_ref[:, rows] = grad_low
        out_ref[rows, :] = dot(query, grad_low, (0, 0)).astype(low)
        if i == 0:
            out_ref[per_quarter * DH :, :] = jnp.zeros((EXTRA, DH), low)
        put_pair(out_ref, per_quarter, i, gain_term)


def times_weight(place, side, normed, weight_ref, start, count):
    width = normed[0].shape[1]
    half = weight_ref.shape[1] // 2
    columns = pl.ds(pl.multiple_of(side * half + start, DH), count)
    total = None
    for j in range(QUAD):
        rows = pl.ds(pl.multiple_of(((place & (QUAD - 1)) ^ j) * width, DH), width)
        part = dot(normed[j][...], weight_ref[rows, columns], (1, 0))
        total = part if total is None else total + part
    return total


def query_kernel(per_quarter, place_ref, side_ref, key_ref, value_ref, weight_ref, *rest):
    lows, normed, prefix = rest[:QUAD], rest[QUAD : 2 * QUAD], rest[2 * QUAD : 3 * QUAD]
    grad_query_hbm, sent_ref, grad_score_ref, grad_query_ref, sems = rest[3 * QUAD :]
    keep = causal(key_ref.shape[0])
    for j, i, head in head_slices(place_ref[0], per_quarter):
        rows = slice(i * DH, (i + 1) * DH)
        raw = dot(lows[j][:, rows], value_ref[:, head], (1, 1))
        grad_scores = jnp.where(keep, raw, 0.0).astype(low)
        grad_score_ref[j * per_quarter + i] = grad_scores
        grad_query = dot(grad_scores, key_ref[:, head], (1, 0))
        grad_query = grad_query + dot(lows[j][:, rows], prefix[j][rows, :], (1, 1))
        grad_query_ref[:, head] = grad_query.astype(low)
    store = pltpu.make_async_copy(grad_query_ref, grad_query_hbm, sems.at[0])
    store.start()
    for start in range(0, sent_ref.shape[1], CHUNK):
        total = times_weight(place_ref[0], 1 - side_ref[0], normed, weight_ref, start, CHUNK)
        sent_ref[:, start : start + CHUNK] = total.astype(low)
    store.wait()


def mixed_kernel(per_quarter, place_ref, side_ref, query_ref, score_ref, grad_score_ref, weight_ref, other_ref, *rest):
    lows, normed, rest = rest[:QUAD], rest[QUAD : 2 * QUAD], rest[2 * QUAD :]
    mixed_hbm, grad_key_ref, grad_value_ref, mixed_ref, sems = rest
    for start in range(0, other_ref.shape[1], CHUNK):
        columns = slice(start, start + CHUNK)
        total = times_weight(place_ref[0], side_ref[0], normed, weight_ref, start, CHUNK)
        mixed_ref[:, columns] = (total + other_ref[:, columns].astype(wide)).astype(low)
    store = pltpu.make_async_copy(mixed_ref, mixed_hbm, sems.at[0])
    store.start()
    for j, i, head in head_slices(place_ref[0], per_quarter):
        n = j * per_quarter + i
        columns = slice(n * DH, (n + 1) * DH)
        scores = score_ref[((place_ref[0] & (QUAD - 1)) ^ j) * per_quarter + i]
        grad_key_ref[:, columns] = dot(grad_score_ref[n], query_ref[:, head], (0, 0))
        grad_value_ref[:, columns] = dot(scores, lows[j][:, i * DH : (i + 1) * DH], (0, 0))
    store.wait()


def finish_kernel(per_quarter, quarters, place_ref, key_ref, value_ref, local_key_ref, local_value_ref, *rest):
    suffix, rest = rest[: len(quarters)], rest[len(quarters) :]
    grad_key_hbm, grad_value_hbm, gain_ref, key_out, value_out, sems = rest[-6:]
    gain_ref[...] = rest[0][...] if len(rest) > 6 else jnp.zeros_like(gain_ref)
    copies = []
    for n, (j, i, head) in enumerate(head_slices(place_ref[0], per_quarter, quarters)):
        rows = slice(i * DH, (i + 1) * DH)
        columns = slice(n * DH, (n + 1) * DH)
        own = slice((j * per_quarter + i) * DH, (j * per_quarter + i + 1) * DH)
        state_ref = suffix[n // per_quarter]
        state = state_ref[rows, :]
        grad_key = local_key_ref[:, own] + dot(value_ref[:, head], state, (1, 1))
        key_out[:, columns] = grad_key.astype(low)
        grad_value = local_value_ref[:, own] + dot(key_ref[:, head], state, (1, 0))
        value_out[:, columns] = grad_value.astype(low)
        copies.append(pltpu.make_async_copy(key_out.at[:, columns], grad_key_hbm.at[:, head], sems.at[0, n]))
        copies.append(pltpu.make_async_copy(value_out.at[:, columns], grad_value_hbm.at[:, head], sems.at[1, n]))
        for copy in copies[-2:]:
            copy.start()
        gain_ref[:, head] = pair_sum(state_ref, per_quarter, i)
    for copy in copies:
        copy.wait()


def pair_sum(ref, per_quarter, i):
    base = per_quarter * DH + 2 * i
    return ref[base : base + 1, :].astype(wide) + ref[base + 1 : base + 2, :].astype(wide)


def put_pair(ref, per_quarter, i, gain):
    base = per_quarter * DH + 2 * i
    upper = gain.astype(low)
    ref[base : base + 1, :] = upper
    ref[base + 1 : base + 2, :] = (gain - upper.astype(wide)).astype(low)


def back_kernel(side_ref, own_hbm, other_ref, weight_hbm, out_ref, weight_ref, own_ref, own_sem, sems):
    width = own_ref.shape[1]
    own = pl.ds(pl.multiple_of(side_ref[0] * width, DH), width)
    other = pl.ds(pl.multiple_of((1 - side_ref[0]) * width, DH), width)
    own_copy = pltpu.make_async_copy(own_hbm, own_ref, own_sem.at[0])
    own_copy.start()
    chunks = [slice(start, start + CHUNK) for start in range(0, weight_ref.shape[0], CHUNK)]
    copies = [
        pltpu.make_async_copy(weight_hbm.at[rows, :], weight_ref.at[rows, :], sems.at[c])
        for c, rows in enumerate(chunks)
    ]
    for copy in copies:
        copy.start()
    own_copy.wait()
    for copy, rows in zip(copies, chunks):
        copy.wait()
        total = dot(own_ref[...], weight_ref[rows, own], (1, 1))
        out_ref[:, rows] = total + dot(other_ref[...], weight_ref[rows, other], (1, 1))


def first_kernel(gains, keep, b0, b1, b2, b3, send_ref, *refs):
    rows = send_ref.shape[0] - (EXTRA if gains else 0)
    blocks = (b0, b1, b2, b3)
    total = sum(block[:rows, :].astype(wide) for block in blocks)
    send_ref[:rows, :] = total.astype(low)
    gain_refs = refs[keep:]
    if keep:
        refs[0][...] = total
    spread_gain(gains, send_ref, gain_refs, blocks, None)


def spread_gain(gains, send_ref, gain_refs, blocks, earlier):
    if not gains:
        return
    send_ref[gains * DH :, :] = jnp.zeros((EXTRA, DH), low)
    for i in range(gains):
        gain = sum(pair_sum(block, gains, i) for block in blocks)
        if earlier is not None:
            gain = gain + earlier[i : i + 1, :]
        gain_refs[0][i : i + 1, :] = gain
        put_pair(send_ref, gains, i, gain)


def is_beyond(place_ref, step, backward):
    return (place_ref[0] & step) == (0 if backward else step)


def step_kernel(gains, past, step, backward, place_ref, total_ref, got_ref, *refs):
    refs = list(refs)
    outside_ref = refs.pop(0) if past else None
    earlier = refs.pop(0) if gains else None
    total_out, outside_out, send_ref = refs[:3]
    rows = total_ref.shape[0]
    state = got_ref[:rows, :].astype(wide)
    outside = jnp.where(is_beyond(place_ref, step, backward), state, 0.0)
    outside_out[...] = outside + outside_ref[...] if past else outside
    total = total_ref[...] + state
    total_out[...] = total
    send_ref[:rows, :] = total.astype(low)
    spread_gain(gains, send_ref, refs[3:], (got_ref,), earlier)


def last_kernel(gains, past, step, backward, place_ref, b0, b1, b2, b3, got_ref, *refs):
    refs = list(refs)
    outside_ref = refs.pop(0) if past else None
    earlier = refs.pop(0) if gains else None
    blocks = (b0, b1, b2, b3)
    rows = got_ref.shape[0] - (EXTRA if gains else 0)
    quarter = place_ref[0] & (QUAD - 1)
    outside = jnp.where(is_beyond(place_ref, step, backward), got_ref[:rows, :].astype(wide), 0.0)
    if past:
        outside = outside + outside_ref[...]
    states = [block[:rows, :].astype(wide) for block in blocks]
    for j in range(QUAD):
        result = outside
        for i in range(QUAD):
            if i == j:
                continue
            source, target = quarter ^ i, quarter ^ j
            counts = (source > target) if backward else (source < target)
            result = result + jnp.where(counts, states[i], 0.0)
        refs[j][:rows, :] = result.astype(low)
        if gains:
            refs[j][rows:, :] = jnp.zeros((EXTRA, DH), low)
    for i in range(gains):
        gain = earlier[i : i + 1, :] + pair_sum(got_ref, gains, i)
        for j in range(QUAD):
            put_pair(refs[j], gains, i, gain)


def swap(array, flip):
    count = lax.axis_size("seq")
    return lax.ppermute(array, "seq", [(i, i ^ flip) for i in range(count)])


def trade(array):
    return lax.ppermute(array, "tensor", [(0, 1), (1, 0)])


def scan(where, parts, backward, rows, gains, before_first, before_last):
    blocks, before_first = begin(parts, before_first)
    back, before_last = end(where, blocks, backward, rows, gains, before_last)
    return back, before_first, before_last


def begin(parts, before_first):
    blocks = [parts[0]] + [swap(parts[j], j) for j in range(1, QUAD)]
    return lax.optimization_barrier((blocks, before_first))


def end(where, blocks, backward, rows, gains, before_last):
    count = lax.axis_size("seq")
    total_shape = [shaped((rows, DH), wide)]
    part_shape = [shaped(blocks[0].shape, low)]
    gain_shape = [shaped((gains, DH), wide)] if gains else []
    keep = int(count > 2 * QUAD)
    send, *rest = call(
        functools.partial(first_kernel, gains, keep),
        part_shape + total_shape * keep + gain_shape,
        [VMEM] * QUAD,
    )(*blocks)
    total, gain = rest[:keep], rest[keep:]
    outside = []
    step = QUAD
    while True:
        got = swap(send, step)
        if 2 * step >= count:
            break
        new_total, new_outside, send, *gain = call(
            functools.partial(step_kernel, gains, len(outside), step, backward),
            total_shape * 2 + part_shape + gain_shape,
            [SMEM] + [VMEM] * (2 + len(outside) + len(gain)),
        )(where, *total, got, *outside, *gain)
        total, outside = [new_total], [new_outside]
        step *= 2
    got, before_last = lax.optimization_barrier((got, before_last))
    results = call(
        functools.partial(last_kernel, gains, len(outside), step, backward),
        part_shape * QUAD,
        [SMEM] + [VMEM] * (QUAD + 1 + len(outside) + len(gain)),
    )(where, *blocks, got, *outside, *gain)
    back = [results[0]] + [swap(results[j], j) for j in range(1, QUAD)]
    return back, before_last


def on_device(queries, key_vectors, values, out_weight, norm_gain, grad_output):
    tokens, width = queries.shape
    model = out_weight.shape[1]
    heads = width // DH
    per_quarter = heads // QUAD
    rows = per_quarter * DH
    place = lax.axis_index("seq")
    where = place.astype(jnp.int32).reshape(1)
    side = lax.axis_index("tensor").astype(jnp.int32).reshape(1)
    gain_row = norm_gain.reshape(1, width)
    whole = shaped((tokens, width), wide)
    whole_low = shaped((tokens, width), low)
    half = model // 2
    result_whole = pltpu.VMEM((tokens, width), low)
    one_sem = pltpu.SemaphoreType.DMA((1,))
    two_sems = pltpu.SemaphoreType.DMA((2,))

    other_grad = trade(grad_output)
    *parts, key_near, value_near = call(
        functools.partial(state_kernel, per_quarter),
        [shaped((rows, DH), low)] * QUAD + [whole_low, whole_low],
        [SMEM, HBM, HBM],
        scratch=[two_sems],
    )(where, key_vectors, values)
    squares = shaped((heads, tokens, tokens), low)
    local, query_near, scores = call(
        functools.partial(local_kernel, heads),
        [whole, whole_low, squares],
        [HBM, VMEM, VMEM],
        scratch=[one_sem],
    )(queries, key_near, value_near)
    grad_normed, weight_near = call(
        back_kernel,
        [whole, shaped(out_weight.shape, low)],
        [SMEM, HBM, VMEM, HBM],
        scratch=[
            pltpu.VMEM((tokens, half), low),
            one_sem,
            pltpu.SemaphoreType.DMA((width // CHUNK,)),
        ],
    )(side, grad_output, other_grad, out_weight)
    prefix, grad_normed, local = scan(where, parts, False, rows, 0, grad_normed, local)

    part_low = shaped((tokens, rows), low)
    normed, lows, terms = zip(
        *(
            call(
                functools.partial(norm_kernel, per_quarter, j),
                [part_low, part_low, shaped((rows + EXTRA, DH), low)],
                [SMEM, VMEM, VMEM, VMEM, FREE, VMEM],
            )(where, query_near, local, grad_normed, gain_row, prefix[j])
            for j in range(QUAD)
        )
    )
    grad_queries, sent, grad_scores = call(
        functools.partial(query_kernel, per_quarter),
        [whole_low, whole_low, squares],
        [SMEM, SMEM] + [VMEM] * (3 + 3 * QUAD),
        out_specs=[HBM, VMEM, VMEM],
        scratch=[result_whole, one_sem],
    )(where, side, key_near, value_near, weight_near, *lows, *normed, *prefix)
    blocks, sent = begin(terms, sent)
    other_part = trade(sent)
    mixed, *local_pair = call(
        functools.partial(mixed_kernel, per_quarter),
        [whole_low, whole, whole],
        [SMEM, SMEM] + [VMEM] * (5 + 2 * QUAD),
        out_specs=[HBM, VMEM, VMEM],
        scratch=[result_whole, one_sem],
    )(where, side, query_near, scores, grad_scores, weight_near, other_part, *lows, *normed)
    suffix, local_pair = end(where, blocks, True, rows, per_quarter, local_pair)

    done = []
    for quarters in FINISH:
        count = len(quarters)
        result = pltpu.VMEM((tokens, count * rows), low)
        grad_keys, grad_values, gain = call(
            functools.partial(finish_kernel, per_quarter, quarters),
            [whole_low, whole_low, shaped((1, width), wide)],
            [SMEM] + [VMEM] * (4 + count) + [VMEM, HBM, HBM][: len(done)],
            out_specs=[HBM, HBM, VMEM if not done else FREE],
            scratch=[result, result, pltpu.SemaphoreType.DMA((2, count * per_quarter))],
            aliases={6 + count: 0, 7 + count: 1} if done else {},
        )(where, key_near, value_near, *local_pair, *(suffix[j] for j in quarters), *done)
        done = [gain, grad_keys, grad_values]
    return mixed, grad_queries, grad_keys, grad_values, gain.reshape(width)


def solution(mesh):
    placed = (
        P(("parts", "seq"), "tensor"),
        P(("parts", "seq"), "tensor"),
        P(("parts", "seq"), "tensor"),
        P("tensor", None),
        P("tensor"),
        P(("parts", "seq"), "tensor"),
    )
    return jax.shard_map(
        on_device,
        mesh=mesh,
        in_specs=placed,
        out_specs=(
            P(("parts", "seq"), "tensor"),
            P(("parts", "seq"), "tensor"),
            P(("parts", "seq"), "tensor"),
            P(("parts", "seq"), "tensor"),
            P(("parts", "tensor")),
        ),
        check_vma=False,
    )
```

```python
import functools

import jax
import jax.numpy as jnp
from jax import lax
from jax.experimental import pallas as pl
from jax.experimental.pallas import tpu as pltpu
from jax.sharding import PartitionSpec as P

DH = 128
QUAD = 4
EXTRA = 16
CHUNK = 512
COST = 1000
FINISH = ((0,), (1, 2, 3))
EPSILON = 1e-05
wide = jnp.float32
low = jnp.bfloat16
VMEM = pl.BlockSpec(memory_space=pltpu.VMEM)
SMEM = pl.BlockSpec(memory_space=pltpu.SMEM)
HBM = pl.BlockSpec(memory_space=pltpu.HBM)
FREE = pl.BlockSpec(memory_space=pltpu.VMEM)


def dot(a, b, over):
    return lax.dot_general(a, b, (((over[0],), (over[1],)), ((), ())), preferred_element_type=wide)


def shaped(shape, dtype):
    return jax.ShapeDtypeStruct(shape, dtype)


def call(body, outs, ins, out_specs=None, scratch=(), room=6, aliases=None):
    out_specs = out_specs or [VMEM] * len(outs)
    placed = [
        pltpu.VMEM(out.shape, out.dtype) if spec is VMEM else out for out, spec in zip(outs, out_specs)
    ]
    kernel = pl.pallas_call(
        body,
        out_shape=placed,
        in_specs=[VMEM if spec is FREE else spec for spec in ins],
        out_specs=[VMEM if spec is FREE else spec for spec in out_specs],
        scratch_shapes=list(scratch),
        input_output_aliases=aliases or {},
        cost_estimate=pl.CostEstimate(flops=COST, bytes_accessed=COST, transcendentals=0),
        compiler_params=pltpu.CompilerParams(vmem_limit_bytes=room * 2**20),
    )

    def pinned(*operands):
        spaces = {id(VMEM): pltpu.VMEM, id(HBM): pltpu.HBM}
        fixed = [
            pltpu.with_memory_space_constraint(operand, spaces[id(spec)]) if id(spec) in spaces else operand
            for operand, spec in zip(operands, ins, strict=True)
        ]
        return kernel(*fixed)

    return pinned


def head_slices(place, per_quarter, quarters=range(QUAD)):
    for j in quarters:
        for i in range(per_quarter):
            start = (((place & (QUAD - 1)) ^ j) * per_quarter + i) * DH
            yield j, i, pl.ds(pl.multiple_of(start, DH), DH)


def state_kernel(per_quarter, place_ref, key_hbm, value_hbm, *rest):
    out_refs, key_ref, value_ref, sems = rest[:QUAD], rest[QUAD], rest[QUAD + 1], rest[QUAD + 2]
    copies = [
        pltpu.make_async_copy(key_hbm, key_ref, sems.at[0]),
        pltpu.make_async_copy(value_hbm, value_ref, sems.at[1]),
    ]
    for copy in copies:
        copy.start()
    for copy in copies:
        copy.wait()
    for j, i, head in head_slices(place_ref[0], per_quarter):
        state = dot(key_ref[:, head], value_ref[:, head], (0, 0))
        out_refs[j][i * DH : (i + 1) * DH, :] = state.astype(low)


def causal(tokens):
    rows = lax.broadcasted_iota(jnp.int32, (tokens, tokens), 0)
    columns = lax.broadcasted_iota(jnp.int32, (tokens, tokens), 1)
    return rows >= columns


def local_kernel(heads, query_hbm, key_ref, value_ref, local_ref, query_ref, score_ref, sems):
    copy = pltpu.make_async_copy(query_hbm, query_ref, sems.at[0])
    copy.start()
    keep = causal(query_ref.shape[0])
    copy.wait()
    for h in range(heads):
        head = slice(h * DH, (h + 1) * DH)
        scores = dot(query_ref[:, head], key_ref[:, head], (1, 1))
        scores = jnp.where(keep, scores, 0.0).astype(low)
        score_ref[h] = scores
        local_ref[:, head] = dot(scores, value_ref[:, head], (1, 0))


def norm_kernel(
    per_quarter, j, place_ref, query_ref, local_ref, grad_ref, gain_ref, prefix_ref,
    normed_ref, low_ref, out_ref
):
    for _, i, head in head_slices(place_ref[0], per_quarter, (j,)):
        rows = slice(i * DH, (i + 1) * DH)
        query = query_ref[:, head]
        attention = local_ref[:, head] + dot(query, prefix_ref[rows, :], (1, 0))
        inverse = lax.rsqrt(jnp.mean(attention * attention, axis=-1, keepdims=True) + EPSILON)
        scaled = attention * inverse
        gain = gain_ref[:, head]
        normed_ref[:, rows] = (scaled * gain).astype(low)
        grad = grad_ref[:, head]
        gain_term = jnp.sum(grad * scaled, axis=0, keepdims=True)
        gained = grad * gain
        inner = jnp.mean(gained * scaled, axis=-1, keepdims=True)
        grad_low = (inverse * (gained - scaled * inner)).astype(low)
        low_ref[:, rows] = grad_low
        out_ref[rows, :] = dot(query, grad_low, (0, 0)).astype(low)
        if i == 0:
            out_ref[per_quarter * DH :, :] = jnp.zeros((EXTRA, DH), low)
        put_pair(out_ref, per_quarter, i, gain_term)


def times_weight(place, side, normed, weight_ref, start, count):
    width = normed[0].shape[1]
    half = weight_ref.shape[1] // 2
    columns = pl.ds(pl.multiple_of(side * half + start, DH), count)
    total = None
    for j in range(QUAD):
        rows = pl.ds(pl.multiple_of(((place & (QUAD - 1)) ^ j) * width, DH), width)
        part = dot(normed[j][...], weight_ref[rows, columns], (1, 0))
        total = part if total is None else total + part
    return total


def query_kernel(per_quarter, place_ref, side_ref, key_ref, value_ref, weight_ref, *rest):
    lows, normed, prefix = rest[:QUAD], rest[QUAD : 2 * QUAD], rest[2 * QUAD : 3 * QUAD]
    grad_query_hbm, sent_ref, grad_score_ref, grad_query_ref, sems = rest[3 * QUAD :]
    keep = causal(key_ref.shape[0])
    for j, i, head in head_slices(place_ref[0], per_quarter):
        rows = slice(i * DH, (i + 1) * DH)
        raw = dot(lows[j][:, rows], value_ref[:, head], (1, 1))
        grad_scores = jnp.where(keep, raw, 0.0).astype(low)
        grad_score_ref[j * per_quarter + i] = grad_scores
        grad_query = dot(grad_scores, key_ref[:, head], (1, 0))
        grad_query = grad_query + dot(lows[j][:, rows], prefix[j][rows, :], (1, 1))
        grad_query_ref[:, head] = grad_query.astype(low)
    store = pltpu.make_async_copy(grad_query_ref, grad_query_hbm, sems.at[0])
    store.start()
    for start in range(0, sent_ref.shape[1], CHUNK):
        total = times_weight(place_ref[0], 1 - side_ref[0], normed, weight_ref, start, CHUNK)
        sent_ref[:, start : start + CHUNK] = total.astype(low)
    store.wait()


def pair_kernel(per_quarter, place_ref, query_ref, score_ref, grad_score_ref, *rest):
    lows, (grad_key_ref, grad_value_ref) = rest[:QUAD], rest[QUAD:]
    for j, i, head in head_slices(place_ref[0], per_quarter):
        n = j * per_quarter + i
        columns = slice(n * DH, (n + 1) * DH)
        scores = score_ref[((place_ref[0] & (QUAD - 1)) ^ j) * per_quarter + i]
        grad_key_ref[:, columns] = dot(grad_score_ref[n], query_ref[:, head], (0, 0))
        grad_value_ref[:, columns] = dot(scores, lows[j][:, i * DH : (i + 1) * DH], (0, 0))


def mixed_kernel(place_ref, side_ref, weight_ref, other_ref, *rest):
    normed, (mixed_hbm, mixed_ref, sems) = rest[:QUAD], rest[QUAD:]
    copies = []
    for n, start in enumerate(range(0, other_ref.shape[1], CHUNK)):
        columns = slice(start, start + CHUNK)
        total = times_weight(place_ref[0], side_ref[0], normed, weight_ref, start, CHUNK)
        mixed_ref[:, columns] = (total + other_ref[:, columns].astype(wide)).astype(low)
        copies.append(pltpu.make_async_copy(mixed_ref.at[:, columns], mixed_hbm.at[:, columns], sems.at[n]))
        copies[n].start()
    for copy in copies:
        copy.wait()


def finish_kernel(per_quarter, quarters, place_ref, key_ref, value_ref, local_key_ref, local_value_ref, *rest):
    suffix, rest = rest[: len(quarters)], rest[len(quarters) :]
    grad_key_hbm, grad_value_hbm, gain_ref, key_out, value_out, sems = rest[-6:]
    gain_ref[...] = rest[0][...] if len(rest) > 6 else jnp.zeros_like(gain_ref)
    copies = []
    for n, (j, i, head) in enumerate(head_slices(place_ref[0], per_quarter, quarters)):
        rows = slice(i * DH, (i + 1) * DH)
        columns = slice(n * DH, (n + 1) * DH)
        own = slice((j * per_quarter + i) * DH, (j * per_quarter + i + 1) * DH)
        state_ref = suffix[n // per_quarter]
        state = state_ref[rows, :]
        grad_key = local_key_ref[:, own] + dot(value_ref[:, head], state, (1, 1))
        key_out[:, columns] = grad_key.astype(low)
        grad_value = local_value_ref[:, own] + dot(key_ref[:, head], state, (1, 0))
        value_out[:, columns] = grad_value.astype(low)
        copies.append(pltpu.make_async_copy(key_out.at[:, columns], grad_key_hbm.at[:, head], sems.at[0, n]))
        copies.append(pltpu.make_async_copy(value_out.at[:, columns], grad_value_hbm.at[:, head], sems.at[1, n]))
        for copy in copies[-2:]:
            copy.start()
        gain_ref[:, head] = pair_sum(state_ref, per_quarter, i)
    for copy in copies:
        copy.wait()


def pair_sum(ref, per_quarter, i):
    base = per_quarter * DH + 2 * i
    return ref[base : base + 1, :].astype(wide) + ref[base + 1 : base + 2, :].astype(wide)


def put_pair(ref, per_quarter, i, gain):
    base = per_quarter * DH + 2 * i
    upper = gain.astype(low)
    ref[base : base + 1, :] = upper
    ref[base + 1 : base + 2, :] = (gain - upper.astype(wide)).astype(low)


def back_kernel(side_ref, own_hbm, other_ref, weight_hbm, out_ref, weight_ref, own_ref, own_sem, sems):
    width = own_ref.shape[1]
    own = pl.ds(pl.multiple_of(side_ref[0] * width, DH), width)
    other = pl.ds(pl.multiple_of((1 - side_ref[0]) * width, DH), width)
    own_copy = pltpu.make_async_copy(own_hbm, own_ref, own_sem.at[0])
    own_copy.start()
    chunks = [slice(start, start + CHUNK) for start in range(0, weight_ref.shape[0], CHUNK)]
    copies = [
        pltpu.make_async_copy(weight_hbm.at[rows, :], weight_ref.at[rows, :], sems.at[c])
        for c, rows in enumerate(chunks)
    ]
    for copy in copies:
        copy.start()
    own_copy.wait()
    for copy, rows in zip(copies, chunks):
        copy.wait()
        total = dot(own_ref[...], weight_ref[rows, own], (1, 1))
        out_ref[:, rows] = total + dot(other_ref[...], weight_ref[rows, other], (1, 1))


def first_kernel(gains, keep, b0, b1, b2, b3, send_ref, *refs):
    rows = send_ref.shape[0] - (EXTRA if gains else 0)
    blocks = (b0, b1, b2, b3)
    total = sum(block[:rows, :].astype(wide) for block in blocks)
    send_ref[:rows, :] = total.astype(low)
    gain_refs = refs[keep:]
    if keep:
        refs[0][...] = total
    spread_gain(gains, send_ref, gain_refs, blocks, None)


def spread_gain(gains, send_ref, gain_refs, blocks, earlier):
    if not gains:
        return
    send_ref[gains * DH :, :] = jnp.zeros((EXTRA, DH), low)
    for i in range(gains):
        gain = sum(pair_sum(block, gains, i) for block in blocks)
        if earlier is not None:
            gain = gain + earlier[i : i + 1, :]
        gain_refs[0][i : i + 1, :] = gain
        put_pair(send_ref, gains, i, gain)


def is_beyond(place_ref, step, backward):
    return (place_ref[0] & step) == (0 if backward else step)


def step_kernel(gains, past, step, backward, place_ref, total_ref, got_ref, *refs):
    refs = list(refs)
    outside_ref = refs.pop(0) if past else None
    earlier = refs.pop(0) if gains else None
    total_out, outside_out, send_ref = refs[:3]
    rows = total_ref.shape[0]
    state = got_ref[:rows, :].astype(wide)
    outside = jnp.where(is_beyond(place_ref, step, backward), state, 0.0)
    outside_out[...] = outside + outside_ref[...] if past else outside
    total = total_ref[...] + state
    total_out[...] = total
    send_ref[:rows, :] = total.astype(low)
    spread_gain(gains, send_ref, refs[3:], (got_ref,), earlier)


def last_kernel(gains, past, step, backward, place_ref, b0, b1, b2, b3, got_ref, *refs):
    refs = list(refs)
    outside_ref = refs.pop(0) if past else None
    earlier = refs.pop(0) if gains else None
    blocks = (b0, b1, b2, b3)
    rows = got_ref.shape[0] - (EXTRA if gains else 0)
    quarter = place_ref[0] & (QUAD - 1)
    outside = jnp.where(is_beyond(place_ref, step, backward), got_ref[:rows, :].astype(wide), 0.0)
    if past:
        outside = outside + outside_ref[...]
    states = [block[:rows, :].astype(wide) for block in blocks]
    for j in range(QUAD):
        result = outside
        for i in range(QUAD):
            if i == j:
                continue
            source, target = quarter ^ i, quarter ^ j
            counts = (source > target) if backward else (source < target)
            result = result + jnp.where(counts, states[i], 0.0)
        refs[j][:rows, :] = result.astype(low)
        if gains:
            refs[j][rows:, :] = jnp.zeros((EXTRA, DH), low)
    for i in range(gains):
        gain = earlier[i : i + 1, :] + pair_sum(got_ref, gains, i)
        for j in range(QUAD):
            put_pair(refs[j], gains, i, gain)


def swap(array, flip):
    count = lax.axis_size("seq")
    return lax.ppermute(array, "seq", [(i, i ^ flip) for i in range(count)])


def trade(array):
    return lax.ppermute(array, "tensor", [(0, 1), (1, 0)])


def scan(where, parts, backward, rows, gains, before_first, before_last):
    blocks, before_first = begin(parts, before_first)
    back, before_last = end(where, blocks, backward, rows, gains, before_last)
    return back, before_first, before_last


def begin(parts, before_first):
    blocks = [parts[0]] + [swap(parts[j], j) for j in range(1, QUAD)]
    return lax.optimization_barrier((blocks, before_first))


def end(where, blocks, backward, rows, gains, before_last):
    count = lax.axis_size("seq")
    total_shape = [shaped((rows, DH), wide)]
    part_shape = [shaped(blocks[0].shape, low)]
    gain_shape = [shaped((gains, DH), wide)] if gains else []
    keep = int(count > 2 * QUAD)
    send, *rest = call(
        functools.partial(first_kernel, gains, keep),
        part_shape + total_shape * keep + gain_shape,
        [VMEM] * QUAD,
    )(*blocks)
    total, gain = rest[:keep], rest[keep:]
    outside = []
    step = QUAD
    while True:
        got = swap(send, step)
        if 2 * step >= count:
            break
        new_total, new_outside, send, *gain = call(
            functools.partial(step_kernel, gains, len(outside), step, backward),
            total_shape * 2 + part_shape + gain_shape,
            [SMEM] + [VMEM] * (2 + len(outside) + len(gain)),
        )(where, *total, got, *outside, *gain)
        total, outside = [new_total], [new_outside]
        step *= 2
    got, before_last = lax.optimization_barrier((got, before_last))
    results = call(
        functools.partial(last_kernel, gains, len(outside), step, backward),
        part_shape * QUAD,
        [SMEM] + [VMEM] * (QUAD + 1 + len(outside) + len(gain)),
    )(where, *blocks, got, *outside, *gain)
    back = [results[0]] + [swap(results[j], j) for j in range(1, QUAD)]
    return back, before_last


def on_device(queries, key_vectors, values, out_weight, norm_gain, grad_output):
    tokens, width = queries.shape
    model = out_weight.shape[1]
    heads = width // DH
    per_quarter = heads // QUAD
    rows = per_quarter * DH
    place = lax.axis_index("seq")
    where = place.astype(jnp.int32).reshape(1)
    side = lax.axis_index("tensor").astype(jnp.int32).reshape(1)
    gain_row = norm_gain.reshape(1, width)
    whole = shaped((tokens, width), wide)
    whole_low = shaped((tokens, width), low)
    half = model // 2
    result_whole = pltpu.VMEM((tokens, width), low)
    one_sem = pltpu.SemaphoreType.DMA((1,))
    two_sems = pltpu.SemaphoreType.DMA((2,))

    other_grad = trade(grad_output)
    *parts, key_near, value_near = call(
        functools.partial(state_kernel, per_quarter),
        [shaped((rows, DH), low)] * QUAD + [whole_low, whole_low],
        [SMEM, HBM, HBM],
        scratch=[two_sems],
    )(where, key_vectors, values)
    squares = shaped((heads, tokens, tokens), low)
    local, query_near, scores = call(
        functools.partial(local_kernel, heads),
        [whole, whole_low, squares],
        [HBM, VMEM, VMEM],
        scratch=[one_sem],
    )(queries, key_near, value_near)
    grad_normed, weight_near = call(
        back_kernel,
        [whole, shaped(out_weight.shape, low)],
        [SMEM, HBM, VMEM, HBM],
        scratch=[
            pltpu.VMEM((tokens, half), low),
            one_sem,
            pltpu.SemaphoreType.DMA((width // CHUNK,)),
        ],
    )(side, grad_output, other_grad, out_weight)
    prefix, grad_normed, local = scan(where, parts, False, rows, 0, grad_normed, local)

    part_low = shaped((tokens, rows), low)
    normed, lows, terms = zip(
        *(
            call(
                functools.partial(norm_kernel, per_quarter, j),
                [part_low, part_low, shaped((rows + EXTRA, DH), low)],
                [SMEM, VMEM, VMEM, VMEM, FREE, VMEM],
            )(where, query_near, local, grad_normed, gain_row, prefix[j])
            for j in range(QUAD)
        )
    )
    grad_queries, sent, grad_scores = call(
        functools.partial(query_kernel, per_quarter),
        [whole_low, whole_low, squares],
        [SMEM, SMEM] + [VMEM] * (3 + 3 * QUAD),
        out_specs=[HBM, VMEM, VMEM],
        scratch=[result_whole, one_sem],
    )(where, side, key_near, value_near, weight_near, *lows, *normed, *prefix)
    blocks, sent = begin(terms, sent)
    local_pair = call(
        functools.partial(pair_kernel, per_quarter),
        [whole, whole],
        [SMEM] + [VMEM] * (3 + QUAD),
    )(where, query_near, scores, grad_scores, *lows)
    suffix, local_pair = end(where, blocks, True, rows, per_quarter, (local_pair, sent))
    local_pair, sent = local_pair
    other_part = trade(sent)
    (mixed,) = call(
        mixed_kernel,
        [whole_low],
        [SMEM, SMEM] + [VMEM] * (2 + QUAD),
        out_specs=[HBM],
        scratch=[result_whole, pltpu.SemaphoreType.DMA((half // CHUNK,))],
    )(where, side, weight_near, other_part, *normed)
    mixed, local_pair = lax.optimization_barrier((mixed, local_pair))

    done = []
    for quarters in FINISH:
        count = len(quarters)
        result = pltpu.VMEM((tokens, count * rows), low)
        grad_keys, grad_values, gain = call(
            functools.partial(finish_kernel, per_quarter, quarters),
            [whole_low, whole_low, shaped((1, width), wide)],
            [SMEM] + [VMEM] * (4 + count) + [VMEM, HBM, HBM][: len(done)],
            out_specs=[HBM, HBM, FREE if quarters is FINISH[-1] else VMEM],
            scratch=[result, result, pltpu.SemaphoreType.DMA((2, count * per_quarter))],
            aliases={6 + count: 0, 7 + count: 1} if done else {},
        )(where, key_near, value_near, *local_pair, *(suffix[j] for j in quarters), *done)
        done = [gain, grad_keys, grad_values]
    return mixed, grad_queries, grad_keys, grad_values, gain.reshape(width)


def solution(mesh):
    placed = (
        P(("parts", "seq"), "tensor"),
        P(("parts", "seq"), "tensor"),
        P(("parts", "seq"), "tensor"),
        P("tensor", None),
        P("tensor"),
        P(("parts", "seq"), "tensor"),
    )
    return jax.shard_map(
        on_device,
        mesh=mesh,
        in_specs=placed,
        out_specs=(
            P(("parts", "seq"), "tensor"),
            P(("parts", "seq"), "tensor"),
            P(("parts", "seq"), "tensor"),
            P(("parts", "seq"), "tensor"),
            P(("parts", "tensor")),
        ),
        check_vma=False,
    )
```

```python
import functools

import jax
import jax.numpy as jnp
from jax import lax
from jax.experimental import pallas as pl
from jax.experimental.pallas import tpu as pltpu
from jax.sharding import PartitionSpec as P

DH = 128
QUAD = 4
EXTRA = 16
CHUNK = 512
COST = 1000
FINISH = (0, 1, 2, 3)
EPSILON = 1e-05
wide = jnp.float32
low = jnp.bfloat16
VMEM = pl.BlockSpec(memory_space=pltpu.VMEM)
SMEM = pl.BlockSpec(memory_space=pltpu.SMEM)
HBM = pl.BlockSpec(memory_space=pltpu.HBM)
FREE = pl.BlockSpec(memory_space=pltpu.VMEM)


def dot(a, b, over):
    return lax.dot_general(a, b, (((over[0],), (over[1],)), ((), ())), preferred_element_type=wide)


def shaped(shape, dtype):
    return jax.ShapeDtypeStruct(shape, dtype)


def call(body, outs, ins, out_specs=None, scratch=(), room=6, aliases=None):
    out_specs = out_specs or [VMEM] * len(outs)
    placed = [
        pltpu.VMEM(out.shape, out.dtype) if spec is VMEM else out for out, spec in zip(outs, out_specs)
    ]
    kernel = pl.pallas_call(
        body,
        out_shape=placed,
        in_specs=[VMEM if spec is FREE else spec for spec in ins],
        out_specs=[VMEM if spec is FREE else spec for spec in out_specs],
        scratch_shapes=list(scratch),
        input_output_aliases=aliases or {},
        cost_estimate=pl.CostEstimate(flops=COST, bytes_accessed=COST, transcendentals=0),
        compiler_params=pltpu.CompilerParams(vmem_limit_bytes=room * 2**20),
    )

    def pinned(*operands):
        spaces = {id(VMEM): pltpu.VMEM, id(HBM): pltpu.HBM}
        fixed = [
            pltpu.with_memory_space_constraint(operand, spaces[id(spec)]) if id(spec) in spaces else operand
            for operand, spec in zip(operands, ins, strict=True)
        ]
        return kernel(*fixed)

    return pinned


def head_slices(place, per_quarter, quarters=range(QUAD)):
    for j in quarters:
        for i in range(per_quarter):
            start = (((place & (QUAD - 1)) ^ j) * per_quarter + i) * DH
            yield j, i, pl.ds(pl.multiple_of(start, DH), DH)


def state_kernel(per_quarter, place_ref, key_hbm, value_hbm, *rest):
    out_refs, key_ref, value_ref, sems = rest[:QUAD], rest[QUAD], rest[QUAD + 1], rest[QUAD + 2]
    copies = [
        pltpu.make_async_copy(key_hbm, key_ref, sems.at[0]),
        pltpu.make_async_copy(value_hbm, value_ref, sems.at[1]),
    ]
    for copy in copies:
        copy.start()
    for copy in copies:
        copy.wait()
    for j, i, head in head_slices(place_ref[0], per_quarter):
        state = dot(key_ref[:, head], value_ref[:, head], (0, 0))
        out_refs[j][i * DH : (i + 1) * DH, :] = state.astype(low)


def causal(tokens):
    rows = lax.broadcasted_iota(jnp.int32, (tokens, tokens), 0)
    columns = lax.broadcasted_iota(jnp.int32, (tokens, tokens), 1)
    return rows >= columns


def local_kernel(heads, query_hbm, key_ref, value_ref, local_ref, query_ref, score_ref, sems):
    copy = pltpu.make_async_copy(query_hbm, query_ref, sems.at[0])
    copy.start()
    keep = causal(query_ref.shape[0])
    copy.wait()
    for h in range(heads):
        head = slice(h * DH, (h + 1) * DH)
        scores = dot(query_ref[:, head], key_ref[:, head], (1, 1))
        scores = jnp.where(keep, scores, 0.0).astype(low)
        score_ref[h] = scores
        local_ref[:, head] = dot(scores, value_ref[:, head], (1, 0))


def norm_kernel(
    per_quarter, j, place_ref, query_ref, local_ref, grad_ref, gain_ref, prefix_ref,
    normed_ref, low_ref, out_ref
):
    for _, i, head in head_slices(place_ref[0], per_quarter, (j,)):
        rows = slice(i * DH, (i + 1) * DH)
        query = query_ref[:, head]
        attention = local_ref[:, head] + dot(query, prefix_ref[rows, :], (1, 0))
        inverse = lax.rsqrt(jnp.mean(attention * attention, axis=-1, keepdims=True) + EPSILON)
        grad = grad_ref[:, head]
        gain = gain_ref[:, head]
        gained = grad * gain
        inner = jnp.mean(gained * attention, axis=-1, keepdims=True)
        cubed = inverse * inverse * inverse
        grad_low = (inverse * gained - attention * (cubed * inner)).astype(low)
        scaled = attention * inverse
        normed_ref[:, rows] = (scaled * gain).astype(low)
        gain_term = jnp.sum(grad * scaled, axis=0, keepdims=True)
        low_ref[:, rows] = grad_low
        out_ref[rows, :] = dot(query, grad_low, (0, 0)).astype(low)
        if i == 0:
            out_ref[per_quarter * DH :, :] = jnp.zeros((EXTRA, DH), low)
        put_pair(out_ref, per_quarter, i, gain_term)


def times_weight(place, side, normed, weight_ref, start, count):
    width = normed[0].shape[1]
    half = weight_ref.shape[1] // 2
    columns = pl.ds(pl.multiple_of(side * half + start, DH), count)
    total = None
    for j in range(QUAD):
        rows = pl.ds(pl.multiple_of(((place & (QUAD - 1)) ^ j) * width, DH), width)
        part = dot(normed[j][...], weight_ref[rows, columns], (1, 0))
        total = part if total is None else total + part
    return total


def query_kernel(per_quarter, place_ref, side_ref, key_ref, value_ref, weight_ref, *rest):
    lows, normed, prefix = rest[:QUAD], rest[QUAD : 2 * QUAD], rest[2 * QUAD : 3 * QUAD]
    grad_query_hbm, sent_ref, grad_score_ref, grad_query_ref, sems = rest[3 * QUAD :]
    keep = causal(key_ref.shape[0])
    for j, i, head in head_slices(place_ref[0], per_quarter):
        rows = slice(i * DH, (i + 1) * DH)
        raw = dot(lows[j][:, rows], value_ref[:, head], (1, 1))
        grad_scores = jnp.where(keep, raw, 0.0).astype(low)
        grad_score_ref[j * per_quarter + i] = grad_scores
        grad_query = dot(grad_scores, key_ref[:, head], (1, 0))
        grad_query = grad_query + dot(lows[j][:, rows], prefix[j][rows, :], (1, 1))
        grad_query_ref[:, head] = grad_query.astype(low)
    store = pltpu.make_async_copy(grad_query_ref, grad_query_hbm, sems.at[0])
    store.start()
    for start in range(0, sent_ref.shape[1], CHUNK):
        total = times_weight(place_ref[0], 1 - side_ref[0], normed, weight_ref, start, CHUNK)
        sent_ref[:, start : start + CHUNK] = total.astype(low)
    store.wait()


def pair_kernel(per_quarter, place_ref, query_ref, score_ref, grad_score_ref, *rest):
    lows, (grad_key_ref, grad_value_ref) = rest[:QUAD], rest[QUAD:]
    for j, i, head in head_slices(place_ref[0], per_quarter):
        n = j * per_quarter + i
        columns = slice(n * DH, (n + 1) * DH)
        scores = score_ref[((place_ref[0] & (QUAD - 1)) ^ j) * per_quarter + i]
        grad_key_ref[:, columns] = dot(grad_score_ref[n], query_ref[:, head], (0, 0))
        grad_value_ref[:, columns] = dot(scores, lows[j][:, i * DH : (i + 1) * DH], (0, 0))


def finish_part(per_quarter, j, place, key_ref, value_ref, local_key_ref, local_value_ref, state_ref, grad_key_ref, grad_value_ref):
    for _, i, head in head_slices(place, per_quarter, (j,)):
        rows = slice(i * DH, (i + 1) * DH)
        own = slice((j * per_quarter + i) * DH, (j * per_quarter + i + 1) * DH)
        state = state_ref[rows, :]
        grad_key = local_key_ref[:, own] + dot(value_ref[:, head], state, (1, 1))
        grad_key_ref[:, rows] = grad_key.astype(low)
        grad_value = local_value_ref[:, own] + dot(key_ref[:, head], state, (1, 0))
        grad_value_ref[:, rows] = grad_value.astype(low)


def finish_kernel(per_quarter, j, place_ref, *refs):
    finish_part(per_quarter, j, place_ref[0], *refs)


def stores(per_quarter, place, quarters, parts, outs, sems):
    width = per_quarter * DH
    copies = []
    for n, part in enumerate(parts):
        start = ((place & (QUAD - 1)) ^ quarters[n // 2]) * width
        columns = pl.ds(pl.multiple_of(start, DH), width)
        copies.append(pltpu.make_async_copy(part, outs[n % 2].at[:, columns], sems.at[n]))
    return copies


def mixed_kernel(per_quarter, quarters, place_ref, side_ref, weight_ref, other_ref, *rest):
    count = 2 * len(quarters)
    normed, parts, rest = rest[:QUAD], rest[QUAD : QUAD + count], rest[QUAD + count :]
    mixed_hbm, grad_key_hbm, grad_value_hbm, mixed_ref, sems = rest
    copies = stores(per_quarter, place_ref[0], quarters, parts, (grad_key_hbm, grad_value_hbm), sems)
    for copy in copies:
        copy.start()
    for start in range(0, other_ref.shape[1], CHUNK):
        columns = slice(start, start + CHUNK)
        total = times_weight(place_ref[0], side_ref[0], normed, weight_ref, start, CHUNK)
        mixed_ref[:, columns] = (total + other_ref[:, columns].astype(wide)).astype(low)
    copies.append(pltpu.make_async_copy(mixed_ref, mixed_hbm, sems.at[count]))
    copies[-1].start()
    for copy in copies:
        copy.wait()


def store_kernel(per_quarter, quarter, place_ref, key_ref, value_ref, local_key_ref, local_value_ref, *rest):
    suffix, rest = rest[:QUAD], rest[QUAD + 2 :]
    grad_key_hbm, grad_value_hbm, gain_hbm, key_part, value_part, gain_ref, sems = rest
    place = place_ref[0]
    for j, i, head in head_slices(place, per_quarter):
        gain_ref[:, head] = pair_sum(suffix[j], per_quarter, i)
    gain_copy = pltpu.make_async_copy(gain_ref, gain_hbm, sems.at[2])
    gain_copy.start()
    finish_part(
        per_quarter, quarter, place, key_ref, value_ref, local_key_ref, local_value_ref, suffix[quarter],
        key_part, value_part,
    )
    copies = stores(per_quarter, place, (quarter,), (key_part, value_part), (grad_key_hbm, grad_value_hbm), sems)
    for copy in copies:
        copy.start()
    for copy in (gain_copy, *copies):
        copy.wait()


def pair_sum(ref, per_quarter, i):
    base = per_quarter * DH + 2 * i
    return ref[base : base + 1, :].astype(wide) + ref[base + 1 : base + 2, :].astype(wide)


def put_pair(ref, per_quarter, i, gain):
    base = per_quarter * DH + 2 * i
    upper = gain.astype(low)
    ref[base : base + 1, :] = upper
    ref[base + 1 : base + 2, :] = (gain - upper.astype(wide)).astype(low)


def back_kernel(side_ref, own_hbm, other_ref, weight_hbm, out_ref, weight_ref, own_ref, own_sem, sems):
    width = own_ref.shape[1]
    own = pl.ds(pl.multiple_of(side_ref[0] * width, DH), width)
    other = pl.ds(pl.multiple_of((1 - side_ref[0]) * width, DH), width)
    own_copy = pltpu.make_async_copy(own_hbm, own_ref, own_sem.at[0])
    own_copy.start()
    chunks = [slice(start, start + CHUNK) for start in range(0, weight_ref.shape[0], CHUNK)]
    copies = [
        pltpu.make_async_copy(weight_hbm.at[rows, :], weight_ref.at[rows, :], sems.at[c])
        for c, rows in enumerate(chunks)
    ]
    for copy in copies:
        copy.start()
    own_copy.wait()
    for copy, rows in zip(copies, chunks):
        copy.wait()
        total = dot(own_ref[...], weight_ref[rows, own], (1, 1))
        out_ref[:, rows] = total + dot(other_ref[...], weight_ref[rows, other], (1, 1))


def first_kernel(gains, keep, b0, b1, b2, b3, send_ref, *refs):
    rows = send_ref.shape[0] - (EXTRA if gains else 0)
    blocks = (b0, b1, b2, b3)
    total = sum(block[:rows, :].astype(wide) for block in blocks)
    send_ref[:rows, :] = total.astype(low)
    gain_refs = refs[keep:]
    if keep:
        refs[0][...] = total
    spread_gain(gains, send_ref, gain_refs, blocks, None)


def spread_gain(gains, send_ref, gain_refs, blocks, earlier):
    if not gains:
        return
    send_ref[gains * DH :, :] = jnp.zeros((EXTRA, DH), low)
    for i in range(gains):
        gain = sum(pair_sum(block, gains, i) for block in blocks)
        if earlier is not None:
            gain = gain + earlier[i : i + 1, :]
        gain_refs[0][i : i + 1, :] = gain
        put_pair(send_ref, gains, i, gain)


def is_beyond(place_ref, step, backward):
    return (place_ref[0] & step) == (0 if backward else step)


def step_kernel(gains, past, step, backward, place_ref, total_ref, got_ref, *refs):
    refs = list(refs)
    outside_ref = refs.pop(0) if past else None
    earlier = refs.pop(0) if gains else None
    total_out, outside_out, send_ref = refs[:3]
    rows = total_ref.shape[0]
    state = got_ref[:rows, :].astype(wide)
    outside = jnp.where(is_beyond(place_ref, step, backward), state, 0.0)
    outside_out[...] = outside + outside_ref[...] if past else outside
    total = total_ref[...] + state
    total_out[...] = total
    send_ref[:rows, :] = total.astype(low)
    spread_gain(gains, send_ref, refs[3:], (got_ref,), earlier)


def last_kernel(gains, past, step, backward, place_ref, b0, b1, b2, b3, got_ref, *refs):
    refs = list(refs)
    outside_ref = refs.pop(0) if past else None
    earlier = refs.pop(0) if gains else None
    blocks = (b0, b1, b2, b3)
    rows = got_ref.shape[0] - (EXTRA if gains else 0)
    quarter = place_ref[0] & (QUAD - 1)
    outside = jnp.where(is_beyond(place_ref, step, backward), got_ref[:rows, :].astype(wide), 0.0)
    if past:
        outside = outside + outside_ref[...]
    states = [block[:rows, :].astype(wide) for block in blocks]
    for j in range(QUAD):
        result = outside
        for i in range(QUAD):
            if i == j:
                continue
            source, target = quarter ^ i, quarter ^ j
            counts = (source > target) if backward else (source < target)
            result = result + jnp.where(counts, states[i], 0.0)
        refs[j][:rows, :] = result.astype(low)
        if gains:
            refs[j][rows:, :] = jnp.zeros((EXTRA, DH), low)
    for i in range(gains):
        gain = earlier[i : i + 1, :] + pair_sum(got_ref, gains, i)
        for j in range(QUAD):
            put_pair(refs[j], gains, i, gain)


def swap(array, flip):
    count = lax.axis_size("seq")
    return lax.ppermute(array, "seq", [(i, i ^ flip) for i in range(count)])


def trade(array):
    return lax.ppermute(array, "tensor", [(0, 1), (1, 0)])


def scan(where, parts, backward, rows, gains, before_first, before_last):
    blocks, before_first = begin(parts, before_first)
    back, before_last = end(where, blocks, backward, rows, gains, before_last)
    return back, before_first, before_last


def begin(parts, before_first):
    blocks = [parts[0]] + [swap(parts[j], j) for j in range(1, QUAD)]
    return lax.optimization_barrier((blocks, before_first))


def end(where, blocks, backward, rows, gains, before_last):
    count = lax.axis_size("seq")
    total_shape = [shaped((rows, DH), wide)]
    part_shape = [shaped(blocks[0].shape, low)]
    gain_shape = [shaped((gains, DH), wide)] if gains else []
    keep = int(count > 2 * QUAD)
    send, *rest = call(
        functools.partial(first_kernel, gains, keep),
        part_shape + total_shape * keep + gain_shape,
        [VMEM] * QUAD,
    )(*blocks)
    total, gain = rest[:keep], rest[keep:]
    outside = []
    step = QUAD
    while True:
        got = swap(send, step)
        if 2 * step >= count:
            break
        new_total, new_outside, send, *gain = call(
            functools.partial(step_kernel, gains, len(outside), step, backward),
            total_shape * 2 + part_shape + gain_shape,
            [SMEM] + [VMEM] * (2 + len(outside) + len(gain)),
        )(where, *total, got, *outside, *gain)
        total, outside = [new_total], [new_outside]
        step *= 2
    got, before_last = lax.optimization_barrier((got, before_last))
    results = call(
        functools.partial(last_kernel, gains, len(outside), step, backward),
        part_shape * QUAD,
        [SMEM] + [VMEM] * (QUAD + 1 + len(outside) + len(gain)),
    )(where, *blocks, got, *outside, *gain)
    back = [results[0]] + [swap(results[j], j) for j in range(1, QUAD)]
    return back, before_last


def on_device(queries, key_vectors, values, out_weight, norm_gain, grad_output):
    tokens, width = queries.shape
    model = out_weight.shape[1]
    heads = width // DH
    per_quarter = heads // QUAD
    rows = per_quarter * DH
    place = lax.axis_index("seq")
    where = place.astype(jnp.int32).reshape(1)
    side = lax.axis_index("tensor").astype(jnp.int32).reshape(1)
    gain_row = norm_gain.reshape(1, width)
    whole = shaped((tokens, width), wide)
    whole_low = shaped((tokens, width), low)
    half = model // 2
    result_whole = pltpu.VMEM((tokens, width), low)
    one_sem = pltpu.SemaphoreType.DMA((1,))
    two_sems = pltpu.SemaphoreType.DMA((2,))

    other_grad = trade(grad_output)
    *parts, key_near, value_near = call(
        functools.partial(state_kernel, per_quarter),
        [shaped((rows, DH), low)] * QUAD + [whole_low, whole_low],
        [SMEM, HBM, HBM],
        scratch=[two_sems],
    )(where, key_vectors, values)
    squares = shaped((heads, tokens, tokens), low)
    local, query_near, scores = call(
        functools.partial(local_kernel, heads),
        [whole, whole_low, squares],
        [HBM, VMEM, VMEM],
        scratch=[one_sem],
    )(queries, key_near, value_near)
    grad_normed, weight_near = call(
        back_kernel,
        [whole, shaped(out_weight.shape, low)],
        [SMEM, HBM, VMEM, HBM],
        scratch=[
            pltpu.VMEM((tokens, half), low),
            one_sem,
            pltpu.SemaphoreType.DMA((width // CHUNK,)),
        ],
    )(side, grad_output, other_grad, out_weight)
    prefix, grad_normed, local = scan(where, parts, False, rows, 0, grad_normed, local)

    part_low = shaped((tokens, rows), low)
    normed, lows, terms = zip(
        *(
            call(
                functools.partial(norm_kernel, per_quarter, j),
                [part_low, part_low, shaped((rows + EXTRA, DH), low)],
                [SMEM, VMEM, VMEM, VMEM, FREE, VMEM],
            )(where, query_near, local, grad_normed, gain_row, prefix[j])
            for j in range(QUAD)
        )
    )
    grad_queries, sent, grad_scores = call(
        functools.partial(query_kernel, per_quarter),
        [whole_low, whole_low, squares],
        [SMEM, SMEM] + [VMEM] * (3 + 3 * QUAD),
        out_specs=[HBM, VMEM, VMEM],
        scratch=[result_whole, one_sem],
    )(where, side, key_near, value_near, weight_near, *lows, *normed, *prefix)
    blocks, sent = begin(terms, sent)
    local_pair = call(
        functools.partial(pair_kernel, per_quarter),
        [whole, whole],
        [SMEM] + [VMEM] * (3 + QUAD),
    )(where, query_near, scores, grad_scores, *lows)
    suffix, local_pair = end(where, blocks, True, rows, per_quarter, (local_pair, sent))
    local_pair, sent = local_pair
    other_part = trade(sent)
    *early, last = FINISH
    finished = []
    for j in early:
        finished += call(
            functools.partial(finish_kernel, per_quarter, j),
            [part_low, part_low],
            [SMEM] + [VMEM] * 5,
        )(where, key_near, value_near, *local_pair, suffix[j])
    mixed, grad_keys, grad_values = call(
        functools.partial(mixed_kernel, per_quarter, early),
        [whole_low, whole_low, whole_low],
        [SMEM, SMEM] + [VMEM] * (2 + QUAD + len(finished)),
        out_specs=[HBM] * 3,
        scratch=[result_whole, pltpu.SemaphoreType.DMA((len(finished) + 1,))],
    )(where, side, weight_near, other_part, *normed, *finished)
    part = pltpu.VMEM((tokens, rows), low)
    grad_keys, grad_values, gain = call(
        functools.partial(store_kernel, per_quarter, last),
        [whole_low, whole_low, shaped((1, width), wide)],
        [SMEM] + [VMEM] * (4 + QUAD) + [HBM, HBM],
        out_specs=[HBM, HBM, HBM],
        scratch=[part, part, pltpu.VMEM((1, width), wide), pltpu.SemaphoreType.DMA((3,))],
        aliases={5 + QUAD: 0, 6 + QUAD: 1},
    )(where, key_near, value_near, *local_pair, *suffix, grad_keys, grad_values)
    return mixed, grad_queries, grad_keys, grad_values, gain.reshape(width)


def solution(mesh):
    placed = (
        P(("parts", "seq"), "tensor"),
        P(("parts", "seq"), "tensor"),
        P(("parts", "seq"), "tensor"),
        P("tensor", None),
        P("tensor"),
        P(("parts", "seq"), "tensor"),
    )
    return jax.shard_map(
        on_device,
        mesh=mesh,
        in_specs=placed,
        out_specs=(
            P(("parts", "seq"), "tensor"),
            P(("parts", "seq"), "tensor"),
            P(("parts", "seq"), "tensor"),
            P(("parts", "seq"), "tensor"),
            P(("parts", "tensor")),
        ),
        check_vma=False,
    )
```

```python
import functools

import jax
import jax.numpy as jnp
from jax import lax
from jax.experimental import pallas as pl
from jax.experimental.pallas import tpu as pltpu
from jax.sharding import PartitionSpec as P

DH = 128
QUAD = 4
EXTRA = 16
CHUNK = 512
COST = 1000
FINISH = (0, 1, 2, 3)
EPSILON = 1e-05
wide = jnp.float32
low = jnp.bfloat16
VMEM = pl.BlockSpec(memory_space=pltpu.VMEM)
SMEM = pl.BlockSpec(memory_space=pltpu.SMEM)
HBM = pl.BlockSpec(memory_space=pltpu.HBM)
FREE = pl.BlockSpec(memory_space=pltpu.VMEM)


def dot(a, b, over):
    return lax.dot_general(a, b, (((over[0],), (over[1],)), ((), ())), preferred_element_type=wide)


def shaped(shape, dtype):
    return jax.ShapeDtypeStruct(shape, dtype)


def call(body, outs, ins, out_specs=None, scratch=(), room=6, aliases=None):
    out_specs = out_specs or [VMEM] * len(outs)
    placed = [
        pltpu.VMEM(out.shape, out.dtype) if spec is VMEM else out for out, spec in zip(outs, out_specs)
    ]
    kernel = pl.pallas_call(
        body,
        out_shape=placed,
        in_specs=[VMEM if spec is FREE else spec for spec in ins],
        out_specs=[VMEM if spec is FREE else spec for spec in out_specs],
        scratch_shapes=list(scratch),
        input_output_aliases=aliases or {},
        cost_estimate=pl.CostEstimate(flops=COST, bytes_accessed=COST, transcendentals=0),
        compiler_params=pltpu.CompilerParams(vmem_limit_bytes=room * 2**20),
    )

    def pinned(*operands):
        spaces = {id(VMEM): pltpu.VMEM, id(HBM): pltpu.HBM}
        fixed = [
            pltpu.with_memory_space_constraint(operand, spaces[id(spec)]) if id(spec) in spaces else operand
            for operand, spec in zip(operands, ins, strict=True)
        ]
        return kernel(*fixed)

    return pinned


def head_slices(place, per_quarter, quarters=range(QUAD)):
    for j in quarters:
        for i in range(per_quarter):
            start = (((place & (QUAD - 1)) ^ j) * per_quarter + i) * DH
            yield j, i, pl.ds(pl.multiple_of(start, DH), DH)


def states(per_quarter, quarters, place, key_ref, value_ref, out_refs):
    for j, i, head in head_slices(place, per_quarter, quarters):
        state = dot(key_ref[:, head], value_ref[:, head], (0, 0))
        out_refs[j - quarters[0]][i * DH : (i + 1) * DH, :] = state.astype(low)


def own_state_kernel(per_quarter, place_ref, key_ref, value_ref, *out_refs):
    states(per_quarter, range(1), place_ref[0], key_ref, value_ref, out_refs)


def state_kernel(per_quarter, place_ref, key_hbm, value_hbm, *rest):
    out_refs, (key_ref, value_ref, sems) = rest[: QUAD - 1], rest[QUAD - 1 :]
    copies = [
        pltpu.make_async_copy(key_hbm, key_ref, sems.at[0]),
        pltpu.make_async_copy(value_hbm, value_ref, sems.at[1]),
    ]
    for copy in copies:
        copy.start()
    for copy in copies:
        copy.wait()
    states(per_quarter, range(1, QUAD), place_ref[0], key_ref, value_ref, out_refs)


def causal(tokens):
    rows = lax.broadcasted_iota(jnp.int32, (tokens, tokens), 0)
    columns = lax.broadcasted_iota(jnp.int32, (tokens, tokens), 1)
    return rows >= columns


def local_kernel(heads, query_hbm, key_ref, value_ref, local_ref, query_ref, score_ref, sems):
    copy = pltpu.make_async_copy(query_hbm, query_ref, sems.at[0])
    copy.start()
    keep = causal(query_ref.shape[0])
    copy.wait()
    for h in range(heads):
        head = slice(h * DH, (h + 1) * DH)
        scores = dot(query_ref[:, head], key_ref[:, head], (1, 1))
        scores = jnp.where(keep, scores, 0.0).astype(low)
        score_ref[h] = scores
        local_ref[:, head] = dot(scores, value_ref[:, head], (1, 0))


def norm_kernel(
    per_quarter, j, place_ref, query_ref, local_ref, grad_ref, gain_ref, prefix_ref,
    normed_ref, low_ref, out_ref
):
    for _, i, head in head_slices(place_ref[0], per_quarter, (j,)):
        rows = slice(i * DH, (i + 1) * DH)
        query = query_ref[:, head]
        attention = local_ref[:, head] + dot(query, prefix_ref[rows, :], (1, 0))
        inverse = lax.rsqrt(jnp.mean(attention * attention, axis=-1, keepdims=True) + EPSILON)
        grad = grad_ref[:, head]
        gain = gain_ref[:, head]
        gained = grad * gain
        inner = jnp.mean(gained * attention, axis=-1, keepdims=True)
        cubed = inverse * inverse * inverse
        grad_low = (inverse * gained - attention * (cubed * inner)).astype(low)
        scaled = attention * inverse
        normed_ref[:, rows] = (scaled * gain).astype(low)
        gain_term = jnp.sum(grad * scaled, axis=0, keepdims=True)
        low_ref[:, rows] = grad_low
        out_ref[rows, :] = dot(query, grad_low, (0, 0)).astype(low)
        if i == 0:
            out_ref[per_quarter * DH :, :] = jnp.zeros((EXTRA, DH), low)
        put_pair(out_ref, per_quarter, i, gain_term)


def times_weight(place, side, normed, weight_ref, start, count):
    width = normed[0].shape[1]
    half = weight_ref.shape[1] // 2
    columns = pl.ds(pl.multiple_of(side * half + start, DH), count)
    total = None
    for j in range(QUAD):
        rows = pl.ds(pl.multiple_of(((place & (QUAD - 1)) ^ j) * width, DH), width)
        part = dot(normed[j][...], weight_ref[rows, columns], (1, 0))
        total = part if total is None else total + part
    return total


def query_kernel(per_quarter, place_ref, side_ref, key_ref, value_ref, weight_ref, *rest):
    lows, normed, prefix = rest[:QUAD], rest[QUAD : 2 * QUAD], rest[2 * QUAD : 3 * QUAD]
    grad_query_hbm, sent_ref, grad_score_ref, grad_query_ref, sems = rest[3 * QUAD :]
    keep = causal(key_ref.shape[0])
    for j, i, head in head_slices(place_ref[0], per_quarter):
        rows = slice(i * DH, (i + 1) * DH)
        raw = dot(lows[j][:, rows], value_ref[:, head], (1, 1))
        grad_scores = jnp.where(keep, raw, 0.0).astype(low)
        grad_score_ref[j * per_quarter + i] = grad_scores
        grad_query = dot(grad_scores, key_ref[:, head], (1, 0))
        grad_query = grad_query + dot(lows[j][:, rows], prefix[j][rows, :], (1, 1))
        grad_query_ref[:, head] = grad_query.astype(low)
    store = pltpu.make_async_copy(grad_query_ref, grad_query_hbm, sems.at[0])
    store.start()
    for start in range(0, sent_ref.shape[1], CHUNK):
        total = times_weight(place_ref[0], 1 - side_ref[0], normed, weight_ref, start, CHUNK)
        sent_ref[:, start : start + CHUNK] = total.astype(low)
    store.wait()


def pair_kernel(per_quarter, place_ref, query_ref, score_ref, grad_score_ref, *rest):
    lows, (grad_key_ref, grad_value_ref) = rest[:QUAD], rest[QUAD:]
    for j, i, head in head_slices(place_ref[0], per_quarter):
        n = j * per_quarter + i
        columns = slice(n * DH, (n + 1) * DH)
        scores = score_ref[((place_ref[0] & (QUAD - 1)) ^ j) * per_quarter + i]
        grad_key_ref[:, columns] = dot(grad_score_ref[n], query_ref[:, head], (0, 0))
        grad_value_ref[:, columns] = dot(scores, lows[j][:, i * DH : (i + 1) * DH], (0, 0))


def finish_part(per_quarter, j, place, key_ref, value_ref, local_key_ref, local_value_ref, state_ref, grad_key_ref, grad_value_ref):
    for _, i, head in head_slices(place, per_quarter, (j,)):
        rows = slice(i * DH, (i + 1) * DH)
        own = slice((j * per_quarter + i) * DH, (j * per_quarter + i + 1) * DH)
        state = state_ref[rows, :]
        grad_key = local_key_ref[:, own] + dot(value_ref[:, head], state, (1, 1))
        grad_key_ref[:, rows] = grad_key.astype(low)
        grad_value = local_value_ref[:, own] + dot(key_ref[:, head], state, (1, 0))
        grad_value_ref[:, rows] = grad_value.astype(low)


def finish_kernel(per_quarter, j, place_ref, *refs):
    finish_part(per_quarter, j, place_ref[0], *refs)


def stores(per_quarter, place, quarters, parts, outs, sems):
    width = per_quarter * DH
    copies = []
    for n, part in enumerate(parts):
        start = ((place & (QUAD - 1)) ^ quarters[n // 2]) * width
        columns = pl.ds(pl.multiple_of(start, DH), width)
        copies.append(pltpu.make_async_copy(part, outs[n % 2].at[:, columns], sems.at[n]))
    return copies


def mixed_kernel(per_quarter, quarters, place_ref, side_ref, weight_ref, other_ref, *rest):
    count = 2 * len(quarters)
    normed, parts, rest = rest[:QUAD], rest[QUAD : QUAD + count], rest[QUAD + count :]
    mixed_hbm, grad_key_hbm, grad_value_hbm, mixed_ref, sems = rest
    copies = stores(per_quarter, place_ref[0], quarters, parts, (grad_key_hbm, grad_value_hbm), sems)
    for copy in copies:
        copy.start()
    for start in range(0, other_ref.shape[1], CHUNK):
        columns = slice(start, start + CHUNK)
        total = times_weight(place_ref[0], side_ref[0], normed, weight_ref, start, CHUNK)
        mixed_ref[:, columns] = (total + other_ref[:, columns].astype(wide)).astype(low)
    copies.append(pltpu.make_async_copy(mixed_ref, mixed_hbm, sems.at[count]))
    copies[-1].start()
    for copy in copies:
        copy.wait()


def store_kernel(per_quarter, quarter, place_ref, key_ref, value_ref, local_key_ref, local_value_ref, *rest):
    suffix, rest = rest[:QUAD], rest[QUAD + 2 :]
    grad_key_hbm, grad_value_hbm, gain_hbm, key_part, value_part, gain_ref, sems = rest
    place = place_ref[0]
    for j, i, head in head_slices(place, per_quarter):
        gain_ref[:, head] = pair_sum(suffix[j], per_quarter, i)
    gain_copy = pltpu.make_async_copy(gain_ref, gain_hbm, sems.at[2])
    gain_copy.start()
    finish_part(
        per_quarter, quarter, place, key_ref, value_ref, local_key_ref, local_value_ref, suffix[quarter],
        key_part, value_part,
    )
    copies = stores(per_quarter, place, (quarter,), (key_part, value_part), (grad_key_hbm, grad_value_hbm), sems)
    for copy in copies:
        copy.start()
    for copy in (gain_copy, *copies):
        copy.wait()


def pair_sum(ref, per_quarter, i):
    base = per_quarter * DH + 2 * i
    return ref[base : base + 1, :].astype(wide) + ref[base + 1 : base + 2, :].astype(wide)


def put_pair(ref, per_quarter, i, gain):
    base = per_quarter * DH + 2 * i
    upper = gain.astype(low)
    ref[base : base + 1, :] = upper
    ref[base + 1 : base + 2, :] = (gain - upper.astype(wide)).astype(low)


def back_kernel(side_ref, own_hbm, other_ref, weight_hbm, out_ref, weight_ref, own_ref, own_sem, sems):
    width = own_ref.shape[1]
    own = pl.ds(pl.multiple_of(side_ref[0] * width, DH), width)
    other = pl.ds(pl.multiple_of((1 - side_ref[0]) * width, DH), width)
    own_copy = pltpu.make_async_copy(own_hbm, own_ref, own_sem.at[0])
    own_copy.start()
    chunks = [slice(start, start + CHUNK) for start in range(0, weight_ref.shape[0], CHUNK)]
    copies = [
        pltpu.make_async_copy(weight_hbm.at[rows, :], weight_ref.at[rows, :], sems.at[c])
        for c, rows in enumerate(chunks)
    ]
    for copy in copies:
        copy.start()
    own_copy.wait()
    for copy, rows in zip(copies, chunks):
        copy.wait()
        total = dot(own_ref[...], weight_ref[rows, own], (1, 1))
        out_ref[:, rows] = total + dot(other_ref[...], weight_ref[rows, other], (1, 1))


def first_kernel(gains, keep, b0, b1, b2, b3, send_ref, *refs):
    rows = send_ref.shape[0] - (EXTRA if gains else 0)
    blocks = (b0, b1, b2, b3)
    total = sum(block[:rows, :].astype(wide) for block in blocks)
    send_ref[:rows, :] = total.astype(low)
    gain_refs = refs[keep:]
    if keep:
        refs[0][...] = total
    spread_gain(gains, send_ref, gain_refs, blocks, None)


def spread_gain(gains, send_ref, gain_refs, blocks, earlier):
    if not gains:
        return
    send_ref[gains * DH :, :] = jnp.zeros((EXTRA, DH), low)
    for i in range(gains):
        gain = sum(pair_sum(block, gains, i) for block in blocks)
        if earlier is not None:
            gain = gain + earlier[i : i + 1, :]
        gain_refs[0][i : i + 1, :] = gain
        put_pair(send_ref, gains, i, gain)


def is_beyond(place_ref, step, backward):
    return (place_ref[0] & step) == (0 if backward else step)


def step_kernel(gains, past, step, backward, place_ref, total_ref, got_ref, *refs):
    refs = list(refs)
    outside_ref = refs.pop(0) if past else None
    earlier = refs.pop(0) if gains else None
    total_out, outside_out, send_ref = refs[:3]
    rows = total_ref.shape[0]
    state = got_ref[:rows, :].astype(wide)
    outside = jnp.where(is_beyond(place_ref, step, backward), state, 0.0)
    outside_out[...] = outside + outside_ref[...] if past else outside
    total = total_ref[...] + state
    total_out[...] = total
    send_ref[:rows, :] = total.astype(low)
    spread_gain(gains, send_ref, refs[3:], (got_ref,), earlier)


def last_kernel(gains, past, step, backward, place_ref, b0, b1, b2, b3, got_ref, *refs):
    refs = list(refs)
    outside_ref = refs.pop(0) if past else None
    earlier = refs.pop(0) if gains else None
    blocks = (b0, b1, b2, b3)
    rows = got_ref.shape[0] - (EXTRA if gains else 0)
    outside = jnp.where(is_beyond(place_ref, step, backward), got_ref[:rows, :].astype(wide), 0.0)
    if past:
        outside = outside + outside_ref[...]
    states = [block[:rows, :].astype(wide) for block in blocks]
    pairs = (states[0] + states[1], states[2] + states[3])
    near = ((place_ref[0] & 1) != 0) != backward
    far = ((place_ref[0] & 2) != 0) != backward
    bases = (
        outside + jnp.where(far, pairs[1], 0.0),
        outside + jnp.where(far, 0.0, pairs[0]),
    )
    for j in range(QUAD):
        neighbour = states[j ^ 1]
        own = jnp.where(near, 0.0, neighbour) if j & 1 else jnp.where(near, neighbour, 0.0)
        result = bases[j >> 1] + own
        refs[j][:rows, :] = result.astype(low)
        if gains:
            refs[j][rows:, :] = jnp.zeros((EXTRA, DH), low)
    for i in range(gains):
        gain = earlier[i : i + 1, :] + pair_sum(got_ref, gains, i)
        for j in range(QUAD):
            put_pair(refs[j], gains, i, gain)


def swap(array, flip):
    count = lax.axis_size("seq")
    return lax.ppermute(array, "seq", [(i, i ^ flip) for i in range(count)])


def trade(array):
    return lax.ppermute(array, "tensor", [(0, 1), (1, 0)])


def scan(where, parts, backward, rows, gains, before_first, before_last):
    blocks, before_first = begin(parts, before_first)
    back, before_last = end(where, blocks, backward, rows, gains, before_last)
    return back, before_first, before_last


def begin(parts, before_first):
    blocks = [parts[0]] + [swap(parts[j], j) for j in range(1, QUAD)]
    return lax.optimization_barrier((blocks, before_first))


def end(where, blocks, backward, rows, gains, before_last):
    count = lax.axis_size("seq")
    total_shape = [shaped((rows, DH), wide)]
    part_shape = [shaped(blocks[0].shape, low)]
    gain_shape = [shaped((gains, DH), wide)] if gains else []
    keep = int(count > 2 * QUAD)
    send, *rest = call(
        functools.partial(first_kernel, gains, keep),
        part_shape + total_shape * keep + gain_shape,
        [VMEM] * QUAD,
    )(*blocks)
    total, gain = rest[:keep], rest[keep:]
    outside = []
    step = QUAD
    while True:
        got = swap(send, step)
        if 2 * step >= count:
            break
        new_total, new_outside, send, *gain = call(
            functools.partial(step_kernel, gains, len(outside), step, backward),
            total_shape * 2 + part_shape + gain_shape,
            [SMEM] + [VMEM] * (2 + len(outside) + len(gain)),
        )(where, *total, got, *outside, *gain)
        total, outside = [new_total], [new_outside]
        step *= 2
    got, before_last = lax.optimization_barrier((got, before_last))
    results = call(
        functools.partial(last_kernel, gains, len(outside), step, backward),
        part_shape * QUAD,
        [SMEM] + [VMEM] * (QUAD + 1 + len(outside) + len(gain)),
    )(where, *blocks, got, *outside, *gain)
    back = [results[0]] + [swap(results[j], j) for j in range(1, QUAD)]
    return back, before_last


def on_device(queries, key_vectors, values, out_weight, norm_gain, grad_output):
    tokens, width = queries.shape
    model = out_weight.shape[1]
    heads = width // DH
    per_quarter = heads // QUAD
    rows = per_quarter * DH
    place = lax.axis_index("seq")
    where = place.astype(jnp.int32).reshape(1)
    side = lax.axis_index("tensor").astype(jnp.int32).reshape(1)
    gain_row = norm_gain.reshape(1, width)
    whole = shaped((tokens, width), wide)
    whole_low = shaped((tokens, width), low)
    half = model // 2
    result_whole = pltpu.VMEM((tokens, width), low)
    one_sem = pltpu.SemaphoreType.DMA((1,))
    two_sems = pltpu.SemaphoreType.DMA((2,))

    other_grad = trade(grad_output)
    *parts, key_near, value_near = call(
        functools.partial(state_kernel, per_quarter),
        [shaped((rows, DH), low)] * (QUAD - 1) + [whole_low, whole_low],
        [SMEM, HBM, HBM],
        scratch=[two_sems],
    )(where, key_vectors, values)
    (own_part,) = call(
        functools.partial(own_state_kernel, per_quarter),
        [shaped((rows, DH), low)],
        [SMEM, VMEM, VMEM],
    )(where, key_near, value_near)
    parts = [own_part, *parts]
    squares = shaped((heads, tokens, tokens), low)
    local, query_near, scores = call(
        functools.partial(local_kernel, heads),
        [whole, whole_low, squares],
        [HBM, VMEM, VMEM],
        scratch=[one_sem],
    )(queries, key_near, value_near)
    grad_normed, weight_near = call(
        back_kernel,
        [whole, shaped(out_weight.shape, low)],
        [SMEM, HBM, VMEM, HBM],
        scratch=[
            pltpu.VMEM((tokens, half), low),
            one_sem,
            pltpu.SemaphoreType.DMA((width // CHUNK,)),
        ],
    )(side, grad_output, other_grad, out_weight)
    prefix, grad_normed, local = scan(where, parts, False, rows, 0, grad_normed, local)

    part_low = shaped((tokens, rows), low)
    normed, lows, terms = zip(
        *(
            call(
                functools.partial(norm_kernel, per_quarter, j),
                [part_low, part_low, shaped((rows + EXTRA, DH), low)],
                [SMEM, VMEM, VMEM, VMEM, FREE, VMEM],
            )(where, query_near, local, grad_normed, gain_row, prefix[j])
            for j in range(QUAD)
        )
    )
    grad_queries, sent, grad_scores = call(
        functools.partial(query_kernel, per_quarter),
        [whole_low, whole_low, squares],
        [SMEM, SMEM] + [VMEM] * (3 + 3 * QUAD),
        out_specs=[HBM, VMEM, VMEM],
        scratch=[result_whole, one_sem],
    )(where, side, key_near, value_near, weight_near, *lows, *normed, *prefix)
    blocks, sent = begin(terms, sent)
    local_pair = call(
        functools.partial(pair_kernel, per_quarter),
        [whole, whole],
        [SMEM] + [VMEM] * (3 + QUAD),
    )(where, query_near, scores, grad_scores, *lows)
    suffix, local_pair = end(where, blocks, True, rows, per_quarter, (local_pair, sent))
    local_pair, sent = local_pair
    other_part = trade(sent)
    *early, last = FINISH
    finished = []
    for j in early:
        finished += call(
            functools.partial(finish_kernel, per_quarter, j),
            [part_low, part_low],
            [SMEM] + [VMEM] * 5,
        )(where, key_near, value_near, *local_pair, suffix[j])
    mixed, grad_keys, grad_values = call(
        functools.partial(mixed_kernel, per_quarter, early),
        [whole_low, whole_low, whole_low],
        [SMEM, SMEM] + [VMEM] * (2 + QUAD + len(finished)),
        out_specs=[HBM] * 3,
        scratch=[result_whole, pltpu.SemaphoreType.DMA((len(finished) + 1,))],
    )(where, side, weight_near, other_part, *normed, *finished)
    part = pltpu.VMEM((tokens, rows), low)
    grad_keys, grad_values, gain = call(
        functools.partial(store_kernel, per_quarter, last),
        [whole_low, whole_low, shaped((1, width), wide)],
        [SMEM] + [VMEM] * (4 + QUAD) + [HBM, HBM],
        out_specs=[HBM, HBM, HBM],
        scratch=[part, part, pltpu.VMEM((1, width), wide), pltpu.SemaphoreType.DMA((3,))],
        aliases={5 + QUAD: 0, 6 + QUAD: 1},
    )(where, key_near, value_near, *local_pair, *suffix, grad_keys, grad_values)
    return mixed, grad_queries, grad_keys, grad_values, gain.reshape(width)


def solution(mesh):
    placed = (
        P(("parts", "seq"), "tensor"),
        P(("parts", "seq"), "tensor"),
        P(("parts", "seq"), "tensor"),
        P("tensor", None),
        P("tensor"),
        P(("parts", "seq"), "tensor"),
    )
    return jax.shard_map(
        on_device,
        mesh=mesh,
        in_specs=placed,
        out_specs=(
            P(("parts", "seq"), "tensor"),
            P(("parts", "seq"), "tensor"),
            P(("parts", "seq"), "tensor"),
            P(("parts", "seq"), "tensor"),
            P(("parts", "tensor")),
        ),
        check_vma=False,
    )
```

```python
import functools

import jax
import jax.numpy as jnp
from jax import lax
from jax.experimental import pallas as pl
from jax.experimental.pallas import tpu as pltpu
from jax.sharding import PartitionSpec as P

DH = 128
QUAD = 4
EXTRA = 16
CHUNK = 512
COST = 1000
FINISH = (0, 1, 2, 3)
EPSILON = 1e-05
wide = jnp.float32
low = jnp.bfloat16
VMEM = pl.BlockSpec(memory_space=pltpu.VMEM)
SMEM = pl.BlockSpec(memory_space=pltpu.SMEM)
HBM = pl.BlockSpec(memory_space=pltpu.HBM)
FREE = pl.BlockSpec(memory_space=pltpu.VMEM)


def dot(a, b, over):
    return lax.dot_general(a, b, (((over[0],), (over[1],)), ((), ())), preferred_element_type=wide)


def shaped(shape, dtype):
    return jax.ShapeDtypeStruct(shape, dtype)


def call(body, outs, ins, out_specs=None, scratch=(), room=6, aliases=None):
    out_specs = out_specs or [VMEM] * len(outs)
    placed = [
        pltpu.VMEM(out.shape, out.dtype) if spec is VMEM else out for out, spec in zip(outs, out_specs)
    ]
    kernel = pl.pallas_call(
        body,
        out_shape=placed,
        in_specs=[VMEM if spec is FREE else spec for spec in ins],
        out_specs=[VMEM if spec is FREE else spec for spec in out_specs],
        scratch_shapes=list(scratch),
        input_output_aliases=aliases or {},
        cost_estimate=pl.CostEstimate(flops=COST, bytes_accessed=COST, transcendentals=0),
        compiler_params=pltpu.CompilerParams(vmem_limit_bytes=room * 2**20),
    )

    def pinned(*operands):
        spaces = {id(VMEM): pltpu.VMEM, id(HBM): pltpu.HBM}
        fixed = [
            pltpu.with_memory_space_constraint(operand, spaces[id(spec)]) if id(spec) in spaces else operand
            for operand, spec in zip(operands, ins, strict=True)
        ]
        return kernel(*fixed)

    return pinned


def head_slices(place, per_quarter, quarters=range(QUAD)):
    for j in quarters:
        for i in range(per_quarter):
            start = (((place & (QUAD - 1)) ^ j) * per_quarter + i) * DH
            yield j, i, pl.ds(pl.multiple_of(start, DH), DH)


def states(per_quarter, quarters, place, key_ref, value_ref, out_refs):
    for j, i, head in head_slices(place, per_quarter, quarters):
        state = dot(key_ref[:, head], value_ref[:, head], (0, 0))
        out_refs[j - quarters[0]][i * DH : (i + 1) * DH, :] = state.astype(low)


def state_kernel(per_quarter, place_ref, key_hbm, value_hbm, *rest):
    out_refs, (key_ref, value_ref, sems) = rest[: QUAD - 1], rest[QUAD - 1 :]
    copies = [
        pltpu.make_async_copy(key_hbm, key_ref, sems.at[0]),
        pltpu.make_async_copy(value_hbm, value_ref, sems.at[1]),
    ]
    for copy in copies:
        copy.start()
    for copy in copies:
        copy.wait()
    states(per_quarter, range(1, QUAD), place_ref[0], key_ref, value_ref, out_refs)


def causal(tokens):
    rows = lax.broadcasted_iota(jnp.int32, (tokens, tokens), 0)
    columns = lax.broadcasted_iota(jnp.int32, (tokens, tokens), 1)
    return rows >= columns


def local_kernel(heads, query_hbm, key_ref, value_ref, local_ref, query_ref, score_ref, sems):
    copy = pltpu.make_async_copy(query_hbm, query_ref, sems.at[0])
    copy.start()
    keep = causal(query_ref.shape[0])
    copy.wait()
    for h in range(heads):
        head = slice(h * DH, (h + 1) * DH)
        scores = dot(query_ref[:, head], key_ref[:, head], (1, 1))
        scores = jnp.where(keep, scores, 0.0).astype(low)
        score_ref[h] = scores
        local_ref[:, head] = dot(scores, value_ref[:, head], (1, 0))


def norm_kernel(
    per_quarter, j, place_ref, query_ref, local_ref, grad_ref, gain_ref, prefix_ref,
    normed_ref, low_ref, out_ref
):
    for _, i, head in head_slices(place_ref[0], per_quarter, (j,)):
        rows = slice(i * DH, (i + 1) * DH)
        query = query_ref[:, head]
        attention = local_ref[:, head] + dot(query, prefix_ref[rows, :], (1, 0))
        inverse = lax.rsqrt(jnp.mean(attention * attention, axis=-1, keepdims=True) + EPSILON)
        grad = grad_ref[:, head]
        gain = gain_ref[:, head]
        gained = grad * gain
        inner = jnp.mean(gained * attention, axis=-1, keepdims=True)
        cubed = inverse * inverse * inverse
        grad_low = (inverse * gained - attention * (cubed * inner)).astype(low)
        scaled = attention * inverse
        normed_ref[:, rows] = (scaled * gain).astype(low)
        gain_term = jnp.sum(grad * scaled, axis=0, keepdims=True)
        low_ref[:, rows] = grad_low
        out_ref[rows, :] = dot(query, grad_low, (0, 0)).astype(low)
        if i == 0:
            out_ref[per_quarter * DH :, :] = jnp.zeros((EXTRA, DH), low)
        put_pair(out_ref, per_quarter, i, gain_term)


def times_weight(place, side, normed, weight_ref, start, count):
    width = normed[0].shape[1]
    half = weight_ref.shape[1] // 2
    columns = pl.ds(pl.multiple_of(side * half + start, DH), count)
    total = None
    for j in range(QUAD):
        rows = pl.ds(pl.multiple_of(((place & (QUAD - 1)) ^ j) * width, DH), width)
        part = dot(normed[j][...], weight_ref[rows, columns], (1, 0))
        total = part if total is None else total + part
    return total


def query_kernel(per_quarter, place_ref, side_ref, key_ref, value_ref, weight_ref, *rest):
    lows, normed, prefix = rest[:QUAD], rest[QUAD : 2 * QUAD], rest[2 * QUAD : 3 * QUAD]
    grad_query_hbm, sent_ref, grad_score_ref, grad_query_ref, sems = rest[3 * QUAD :]
    keep = causal(key_ref.shape[0])
    for j, i, head in head_slices(place_ref[0], per_quarter):
        rows = slice(i * DH, (i + 1) * DH)
        raw = dot(lows[j][:, rows], value_ref[:, head], (1, 1))
        grad_scores = jnp.where(keep, raw, 0.0).astype(low)
        grad_score_ref[j * per_quarter + i] = grad_scores
        grad_query = dot(grad_scores, key_ref[:, head], (1, 0))
        grad_query = grad_query + dot(lows[j][:, rows], prefix[j][rows, :], (1, 1))
        grad_query_ref[:, head] = grad_query.astype(low)
    store = pltpu.make_async_copy(grad_query_ref, grad_query_hbm, sems.at[0])
    store.start()
    for start in range(0, sent_ref.shape[1], CHUNK):
        total = times_weight(place_ref[0], 1 - side_ref[0], normed, weight_ref, start, CHUNK)
        sent_ref[:, start : start + CHUNK] = total.astype(low)
    store.wait()


def pair_kernel(per_quarter, place_ref, query_ref, score_ref, grad_score_ref, *rest):
    lows, (grad_key_ref, grad_value_ref) = rest[:QUAD], rest[QUAD:]
    for j, i, head in head_slices(place_ref[0], per_quarter):
        n = j * per_quarter + i
        columns = slice(n * DH, (n + 1) * DH)
        scores = score_ref[((place_ref[0] & (QUAD - 1)) ^ j) * per_quarter + i]
        grad_key_ref[:, columns] = dot(grad_score_ref[n], query_ref[:, head], (0, 0))
        grad_value_ref[:, columns] = dot(scores, lows[j][:, i * DH : (i + 1) * DH], (0, 0))


def finish_part(per_quarter, j, place, key_ref, value_ref, local_key_ref, local_value_ref, state_ref, grad_key_ref, grad_value_ref):
    for _, i, head in head_slices(place, per_quarter, (j,)):
        rows = slice(i * DH, (i + 1) * DH)
        own = slice((j * per_quarter + i) * DH, (j * per_quarter + i + 1) * DH)
        state = state_ref[rows, :]
        grad_key = local_key_ref[:, own] + dot(value_ref[:, head], state, (1, 1))
        grad_key_ref[:, rows] = grad_key.astype(low)
        grad_value = local_value_ref[:, own] + dot(key_ref[:, head], state, (1, 0))
        grad_value_ref[:, rows] = grad_value.astype(low)


def finish_kernel(per_quarter, j, place_ref, *refs):
    finish_part(per_quarter, j, place_ref[0], *refs)


def stores(per_quarter, place, quarters, parts, outs, sems):
    width = per_quarter * DH
    copies = []
    for n, part in enumerate(parts):
        start = ((place & (QUAD - 1)) ^ quarters[n // 2]) * width
        columns = pl.ds(pl.multiple_of(start, DH), width)
        copies.append(pltpu.make_async_copy(part, outs[n % 2].at[:, columns], sems.at[n]))
    return copies


def mixed_kernel(per_quarter, quarters, place_ref, side_ref, weight_ref, other_ref, *rest):
    count = 2 * len(quarters)
    normed, parts, rest = rest[:QUAD], rest[QUAD : QUAD + count], rest[QUAD + count :]
    mixed_hbm, grad_key_hbm, grad_value_hbm, mixed_ref, sems = rest
    copies = stores(per_quarter, place_ref[0], quarters, parts, (grad_key_hbm, grad_value_hbm), sems)
    for copy in copies:
        copy.start()
    for start in range(0, other_ref.shape[1], CHUNK):
        columns = slice(start, start + CHUNK)
        total = times_weight(place_ref[0], side_ref[0], normed, weight_ref, start, CHUNK)
        mixed_ref[:, columns] = (total + other_ref[:, columns].astype(wide)).astype(low)
    copies.append(pltpu.make_async_copy(mixed_ref, mixed_hbm, sems.at[count]))
    copies[-1].start()
    for copy in copies:
        copy.wait()


def store_kernel(per_quarter, quarter, place_ref, key_ref, value_ref, local_key_ref, local_value_ref, *rest):
    suffix, rest = rest[:QUAD], rest[QUAD + 2 :]
    grad_key_hbm, grad_value_hbm, gain_hbm, key_part, value_part, gain_ref, sems = rest
    place = place_ref[0]
    for j, i, head in head_slices(place, per_quarter):
        gain_ref[:, head] = pair_sum(suffix[j], per_quarter, i)
    gain_copy = pltpu.make_async_copy(gain_ref, gain_hbm, sems.at[2])
    gain_copy.start()
    finish_part(
        per_quarter, quarter, place, key_ref, value_ref, local_key_ref, local_value_ref, suffix[quarter],
        key_part, value_part,
    )
    copies = stores(per_quarter, place, (quarter,), (key_part, value_part), (grad_key_hbm, grad_value_hbm), sems)
    for copy in copies:
        copy.start()
    for copy in (gain_copy, *copies):
        copy.wait()


def pair_sum(ref, per_quarter, i):
    base = per_quarter * DH + 2 * i
    return ref[base : base + 1, :].astype(wide) + ref[base + 1 : base + 2, :].astype(wide)


def put_pair(ref, per_quarter, i, gain):
    base = per_quarter * DH + 2 * i
    upper = gain.astype(low)
    ref[base : base + 1, :] = upper
    ref[base + 1 : base + 2, :] = (gain - upper.astype(wide)).astype(low)


def back_kernel(
    per_quarter, side_ref, own_hbm, other_ref, weight_hbm, place_ref, key_ref, value_ref,
    out_ref, weight_ref, part_ref, own_ref, own_sem, sems
):
    width = own_ref.shape[1]
    own = pl.ds(pl.multiple_of(side_ref[0] * width, DH), width)
    other = pl.ds(pl.multiple_of((1 - side_ref[0]) * width, DH), width)
    own_copy = pltpu.make_async_copy(own_hbm, own_ref, own_sem.at[0])
    own_copy.start()
    chunks = [slice(start, start + CHUNK) for start in range(0, weight_ref.shape[0], CHUNK)]
    copies = [
        pltpu.make_async_copy(weight_hbm.at[rows, :], weight_ref.at[rows, :], sems.at[c])
        for c, rows in enumerate(chunks)
    ]
    for copy in copies:
        copy.start()
    states(per_quarter, range(1), place_ref[0], key_ref, value_ref, (part_ref,))
    own_copy.wait()
    for copy, rows in zip(copies, chunks):
        copy.wait()
        total = dot(own_ref[...], weight_ref[rows, own], (1, 1))
        out_ref[:, rows] = total + dot(other_ref[...], weight_ref[rows, other], (1, 1))


def first_kernel(gains, keep, b0, b1, b2, b3, send_ref, *refs):
    rows = send_ref.shape[0] - (EXTRA if gains else 0)
    blocks = (b0, b1, b2, b3)
    total = sum(block[:rows, :].astype(wide) for block in blocks)
    send_ref[:rows, :] = total.astype(low)
    gain_refs = refs[keep:]
    if keep:
        refs[0][...] = total
    spread_gain(gains, send_ref, gain_refs, blocks, None)


def spread_gain(gains, send_ref, gain_refs, blocks, earlier):
    if not gains:
        return
    send_ref[gains * DH :, :] = jnp.zeros((EXTRA, DH), low)
    for i in range(gains):
        gain = sum(pair_sum(block, gains, i) for block in blocks)
        if earlier is not None:
            gain = gain + earlier[i : i + 1, :]
        gain_refs[0][i : i + 1, :] = gain
        put_pair(send_ref, gains, i, gain)


def is_beyond(place_ref, step, backward):
    return (place_ref[0] & step) == (0 if backward else step)


def step_kernel(gains, past, step, backward, place_ref, total_ref, got_ref, *refs):
    refs = list(refs)
    outside_ref = refs.pop(0) if past else None
    earlier = refs.pop(0) if gains else None
    total_out, outside_out, send_ref = refs[:3]
    rows = total_ref.shape[0]
    state = got_ref[:rows, :].astype(wide)
    outside = jnp.where(is_beyond(place_ref, step, backward), state, 0.0)
    outside_out[...] = outside + outside_ref[...] if past else outside
    total = total_ref[...] + state
    total_out[...] = total
    send_ref[:rows, :] = total.astype(low)
    spread_gain(gains, send_ref, refs[3:], (got_ref,), earlier)


def last_kernel(gains, past, step, backward, place_ref, b0, b1, b2, b3, got_ref, *refs):
    refs = list(refs)
    outside_ref = refs.pop(0) if past else None
    earlier = refs.pop(0) if gains else None
    blocks = (b0, b1, b2, b3)
    rows = got_ref.shape[0] - (EXTRA if gains else 0)
    outside = jnp.where(is_beyond(place_ref, step, backward), got_ref[:rows, :].astype(wide), 0.0)
    if past:
        outside = outside + outside_ref[...]
    states = [block[:rows, :].astype(wide) for block in blocks]
    pairs = (states[0] + states[1], states[2] + states[3])
    near = ((place_ref[0] & 1) != 0) != backward
    far = ((place_ref[0] & 2) != 0) != backward
    bases = (
        outside + jnp.where(far, pairs[1], 0.0),
        outside + jnp.where(far, 0.0, pairs[0]),
    )
    for j in range(QUAD):
        neighbour = states[j ^ 1]
        own = jnp.where(near, 0.0, neighbour) if j & 1 else jnp.where(near, neighbour, 0.0)
        result = bases[j >> 1] + own
        refs[j][:rows, :] = result.astype(low)
        if gains:
            refs[j][rows:, :] = jnp.zeros((EXTRA, DH), low)
    for i in range(gains):
        gain = earlier[i : i + 1, :] + pair_sum(got_ref, gains, i)
        for j in range(QUAD):
            put_pair(refs[j], gains, i, gain)


def swap(array, flip):
    count = lax.axis_size("seq")
    return lax.ppermute(array, "seq", [(i, i ^ flip) for i in range(count)])


def trade(array):
    return lax.ppermute(array, "tensor", [(0, 1), (1, 0)])


def scan(where, parts, backward, rows, gains, before_first, before_last):
    blocks, before_first = begin(parts, before_first)
    back, before_last = end(where, blocks, backward, rows, gains, before_last)
    return back, before_first, before_last


def begin(parts, before_first):
    blocks = [parts[0]] + [swap(parts[j], j) for j in range(1, QUAD)]
    return lax.optimization_barrier((blocks, before_first))


def end(where, blocks, backward, rows, gains, before_last):
    count = lax.axis_size("seq")
    total_shape = [shaped((rows, DH), wide)]
    part_shape = [shaped(blocks[0].shape, low)]
    gain_shape = [shaped((gains, DH), wide)] if gains else []
    keep = int(count > 2 * QUAD)
    send, *rest = call(
        functools.partial(first_kernel, gains, keep),
        part_shape + total_shape * keep + gain_shape,
        [VMEM] * QUAD,
    )(*blocks)
    total, gain = rest[:keep], rest[keep:]
    outside = []
    step = QUAD
    while True:
        got = swap(send, step)
        if 2 * step >= count:
            break
        new_total, new_outside, send, *gain = call(
            functools.partial(step_kernel, gains, len(outside), step, backward),
            total_shape * 2 + part_shape + gain_shape,
            [SMEM] + [VMEM] * (2 + len(outside) + len(gain)),
        )(where, *total, got, *outside, *gain)
        total, outside = [new_total], [new_outside]
        step *= 2
    got, before_last = lax.optimization_barrier((got, before_last))
    results = call(
        functools.partial(last_kernel, gains, len(outside), step, backward),
        part_shape * QUAD,
        [SMEM] + [VMEM] * (QUAD + 1 + len(outside) + len(gain)),
    )(where, *blocks, got, *outside, *gain)
    back = [results[0]] + [swap(results[j], j) for j in range(1, QUAD)]
    return back, before_last


def on_device(queries, key_vectors, values, out_weight, norm_gain, grad_output):
    tokens, width = queries.shape
    model = out_weight.shape[1]
    heads = width // DH
    per_quarter = heads // QUAD
    rows = per_quarter * DH
    place = lax.axis_index("seq")
    where = place.astype(jnp.int32).reshape(1)
    side = lax.axis_index("tensor").astype(jnp.int32).reshape(1)
    gain_row = norm_gain.reshape(1, width)
    whole = shaped((tokens, width), wide)
    whole_low = shaped((tokens, width), low)
    half = model // 2
    result_whole = pltpu.VMEM((tokens, width), low)
    one_sem = pltpu.SemaphoreType.DMA((1,))
    two_sems = pltpu.SemaphoreType.DMA((2,))

    other_grad = trade(grad_output)
    *parts, key_near, value_near = call(
        functools.partial(state_kernel, per_quarter),
        [shaped((rows, DH), low)] * (QUAD - 1) + [whole_low, whole_low],
        [SMEM, HBM, HBM],
        scratch=[two_sems],
    )(where, key_vectors, values)
    squares = shaped((heads, tokens, tokens), low)
    local, query_near, scores = call(
        functools.partial(local_kernel, heads),
        [whole, whole_low, squares],
        [HBM, VMEM, VMEM],
        scratch=[one_sem],
    )(queries, key_near, value_near)
    grad_normed, weight_near, own_part = call(
        functools.partial(back_kernel, per_quarter),
        [whole, shaped(out_weight.shape, low), shaped((rows, DH), low)],
        [SMEM, HBM, VMEM, HBM, SMEM, VMEM, VMEM],
        scratch=[
            pltpu.VMEM((tokens, half), low),
            one_sem,
            pltpu.SemaphoreType.DMA((width // CHUNK,)),
        ],
    )(side, grad_output, other_grad, out_weight, where, key_near, value_near)
    parts = [own_part, *parts]
    prefix, grad_normed, local = scan(where, parts, False, rows, 0, grad_normed, local)

    part_low = shaped((tokens, rows), low)
    normed, lows, terms = zip(
        *(
            call(
                functools.partial(norm_kernel, per_quarter, j),
                [part_low, part_low, shaped((rows + EXTRA, DH), low)],
                [SMEM, VMEM, VMEM, VMEM, FREE, VMEM],
            )(where, query_near, local, grad_normed, gain_row, prefix[j])
            for j in range(QUAD)
        )
    )
    grad_queries, sent, grad_scores = call(
        functools.partial(query_kernel, per_quarter),
        [whole_low, whole_low, squares],
        [SMEM, SMEM] + [VMEM] * (3 + 3 * QUAD),
        out_specs=[HBM, VMEM, VMEM],
        scratch=[result_whole, one_sem],
    )(where, side, key_near, value_near, weight_near, *lows, *normed, *prefix)
    blocks, sent = begin(terms, sent)
    local_pair = call(
        functools.partial(pair_kernel, per_quarter),
        [whole, whole],
        [SMEM] + [VMEM] * (3 + QUAD),
    )(where, query_near, scores, grad_scores, *lows)
    suffix, local_pair = end(where, blocks, True, rows, per_quarter, (local_pair, sent))
    local_pair, sent = local_pair
    other_part = trade(sent)
    *early, last = FINISH
    finished = []
    for j in early:
        finished += call(
            functools.partial(finish_kernel, per_quarter, j),
            [part_low, part_low],
            [SMEM] + [VMEM] * 5,
        )(where, key_near, value_near, *local_pair, suffix[j])
    mixed, grad_keys, grad_values = call(
        functools.partial(mixed_kernel, per_quarter, early),
        [whole_low, whole_low, whole_low],
        [SMEM, SMEM] + [VMEM] * (2 + QUAD + len(finished)),
        out_specs=[HBM] * 3,
        scratch=[result_whole, pltpu.SemaphoreType.DMA((len(finished) + 1,))],
    )(where, side, weight_near, other_part, *normed, *finished)
    part = pltpu.VMEM((tokens, rows), low)
    grad_keys, grad_values, gain = call(
        functools.partial(store_kernel, per_quarter, last),
        [whole_low, whole_low, shaped((1, width), wide)],
        [SMEM] + [VMEM] * (4 + QUAD) + [HBM, HBM],
        out_specs=[HBM, HBM, HBM],
        scratch=[part, part, pltpu.VMEM((1, width), wide), pltpu.SemaphoreType.DMA((3,))],
        aliases={5 + QUAD: 0, 6 + QUAD: 1},
    )(where, key_near, value_near, *local_pair, *suffix, grad_keys, grad_values)
    return mixed, grad_queries, grad_keys, grad_values, gain.reshape(width)


def solution(mesh):
    placed = (
        P(("parts", "seq"), "tensor"),
        P(("parts", "seq"), "tensor"),
        P(("parts", "seq"), "tensor"),
        P("tensor", None),
        P("tensor"),
        P(("parts", "seq"), "tensor"),
    )
    return jax.shard_map(
        on_device,
        mesh=mesh,
        in_specs=placed,
        out_specs=(
            P(("parts", "seq"), "tensor"),
            P(("parts", "seq"), "tensor"),
            P(("parts", "seq"), "tensor"),
            P(("parts", "seq"), "tensor"),
            P(("parts", "tensor")),
        ),
        check_vma=False,
    )
```

```python
import functools

import jax
import jax.numpy as jnp
from jax import lax
from jax.experimental import pallas as pl
from jax.experimental.pallas import tpu as pltpu
from jax.sharding import PartitionSpec as P

DH = 128
QUAD = 4
EXTRA = 16
CHUNK = 512
COST = 1000
FINISH = ((0, 1), (2, 3))
EPSILON = 1e-05
wide = jnp.float32
low = jnp.bfloat16
VMEM = pl.BlockSpec(memory_space=pltpu.VMEM)
SMEM = pl.BlockSpec(memory_space=pltpu.SMEM)
HBM = pl.BlockSpec(memory_space=pltpu.HBM)
FREE = pl.BlockSpec(memory_space=pltpu.VMEM)


def dot(a, b, over):
    return lax.dot_general(a, b, (((over[0],), (over[1],)), ((), ())), preferred_element_type=wide)


def shaped(shape, dtype):
    return jax.ShapeDtypeStruct(shape, dtype)


def call(body, outs, ins, out_specs=None, scratch=(), room=6, aliases=None):
    out_specs = out_specs or [VMEM] * len(outs)
    placed = [
        pltpu.VMEM(out.shape, out.dtype) if spec is VMEM else out for out, spec in zip(outs, out_specs)
    ]
    kernel = pl.pallas_call(
        body,
        out_shape=placed,
        in_specs=[VMEM if spec is FREE else spec for spec in ins],
        out_specs=[VMEM if spec is FREE else spec for spec in out_specs],
        scratch_shapes=list(scratch),
        input_output_aliases=aliases or {},
        cost_estimate=pl.CostEstimate(flops=COST, bytes_accessed=COST, transcendentals=0),
        compiler_params=pltpu.CompilerParams(vmem_limit_bytes=room * 2**20),
    )

    def pinned(*operands):
        spaces = {id(VMEM): pltpu.VMEM, id(HBM): pltpu.HBM}
        fixed = [
            pltpu.with_memory_space_constraint(operand, spaces[id(spec)]) if id(spec) in spaces else operand
            for operand, spec in zip(operands, ins, strict=True)
        ]
        return kernel(*fixed)

    return pinned


def head_slices(place, per_quarter, quarters=range(QUAD)):
    for j in quarters:
        for i in range(per_quarter):
            start = (((place & (QUAD - 1)) ^ j) * per_quarter + i) * DH
            yield j, i, pl.ds(pl.multiple_of(start, DH), DH)


def state_kernel(per_quarter, place_ref, key_hbm, value_hbm, *rest):
    out_refs, key_ref, value_ref, sems = rest[:QUAD], rest[QUAD], rest[QUAD + 1], rest[QUAD + 2]
    copies = [
        pltpu.make_async_copy(key_hbm, key_ref, sems.at[0]),
        pltpu.make_async_copy(value_hbm, value_ref, sems.at[1]),
    ]
    for copy in copies:
        copy.start()
    for copy in copies:
        copy.wait()
    for j, i, head in head_slices(place_ref[0], per_quarter):
        state = dot(key_ref[:, head], value_ref[:, head], (0, 0))
        out_refs[j][i * DH : (i + 1) * DH, :] = state.astype(low)


def causal(tokens):
    rows = lax.broadcasted_iota(jnp.int32, (tokens, tokens), 0)
    columns = lax.broadcasted_iota(jnp.int32, (tokens, tokens), 1)
    return rows >= columns


def local_kernel(heads, query_hbm, key_ref, value_ref, local_ref, query_ref, score_ref, sems):
    copy = pltpu.make_async_copy(query_hbm, query_ref, sems.at[0])
    copy.start()
    keep = causal(query_ref.shape[0])
    copy.wait()
    for h in range(heads):
        head = slice(h * DH, (h + 1) * DH)
        scores = dot(query_ref[:, head], key_ref[:, head], (1, 1))
        scores = jnp.where(keep, scores, 0.0).astype(low)
        score_ref[h] = scores
        local_ref[:, head] = dot(scores, value_ref[:, head], (1, 0))


def norm_kernel(
    per_quarter, j, place_ref, query_ref, local_ref, grad_ref, gain_ref, prefix_ref,
    normed_ref, low_ref, out_ref
):
    for _, i, head in head_slices(place_ref[0], per_quarter, (j,)):
        rows = slice(i * DH, (i + 1) * DH)
        query = query_ref[:, head]
        attention = local_ref[:, head] + dot(query, prefix_ref[rows, :], (1, 0))
        inverse = lax.rsqrt(jnp.mean(attention * attention, axis=-1, keepdims=True) + EPSILON)
        grad = grad_ref[:, head]
        gain = gain_ref[:, head]
        gained = grad * gain
        inner = jnp.mean(gained * attention, axis=-1, keepdims=True)
        cubed = inverse * inverse * inverse
        grad_low = (inverse * gained - attention * (cubed * inner)).astype(low)
        scaled = attention * inverse
        normed_ref[:, rows] = (scaled * gain).astype(low)
        gain_term = jnp.sum(grad * scaled, axis=0, keepdims=True)
        low_ref[:, rows] = grad_low
        out_ref[rows, :] = dot(query, grad_low, (0, 0)).astype(low)
        if i == 0:
            out_ref[per_quarter * DH :, :] = jnp.zeros((EXTRA, DH), low)
        put_pair(out_ref, per_quarter, i, gain_term)


def times_weight(place, side, normed, weight_ref, start, count):
    width = normed[0].shape[1]
    half = weight_ref.shape[1] // 2
    columns = pl.ds(pl.multiple_of(side * half + start, DH), count)
    total = None
    for j in range(QUAD):
        rows = pl.ds(pl.multiple_of(((place & (QUAD - 1)) ^ j) * width, DH), width)
        part = dot(normed[j][...], weight_ref[rows, columns], (1, 0))
        total = part if total is None else total + part
    return total


def query_kernel(per_quarter, place_ref, side_ref, key_ref, value_ref, weight_ref, *rest):
    lows, normed, prefix = rest[:QUAD], rest[QUAD : 2 * QUAD], rest[2 * QUAD : 3 * QUAD]
    grad_query_hbm, sent_ref, grad_score_ref, grad_query_ref, sems = rest[3 * QUAD :]
    keep = causal(key_ref.shape[0])
    for j, i, head in head_slices(place_ref[0], per_quarter):
        rows = slice(i * DH, (i + 1) * DH)
        raw = dot(lows[j][:, rows], value_ref[:, head], (1, 1))
        grad_scores = jnp.where(keep, raw, 0.0).astype(low)
        grad_score_ref[j * per_quarter + i] = grad_scores
        grad_query = dot(grad_scores, key_ref[:, head], (1, 0))
        grad_query = grad_query + dot(lows[j][:, rows], prefix[j][rows, :], (1, 1))
        grad_query_ref[:, head] = grad_query.astype(low)
    store = pltpu.make_async_copy(grad_query_ref, grad_query_hbm, sems.at[0])
    store.start()
    for start in range(0, sent_ref.shape[1], CHUNK):
        total = times_weight(place_ref[0], 1 - side_ref[0], normed, weight_ref, start, CHUNK)
        sent_ref[:, start : start + CHUNK] = total.astype(low)
    store.wait()


def pair_kernel(per_quarter, place_ref, query_ref, score_ref, grad_score_ref, *rest):
    lows, (grad_key_ref, grad_value_ref) = rest[:QUAD], rest[QUAD:]
    for j, i, head in head_slices(place_ref[0], per_quarter):
        n = j * per_quarter + i
        columns = slice(n * DH, (n + 1) * DH)
        scores = score_ref[((place_ref[0] & (QUAD - 1)) ^ j) * per_quarter + i]
        grad_key_ref[:, columns] = dot(grad_score_ref[n], query_ref[:, head], (0, 0))
        grad_value_ref[:, columns] = dot(scores, lows[j][:, i * DH : (i + 1) * DH], (0, 0))


def finish_part(per_quarter, j, place, key_ref, value_ref, local_key_ref, local_value_ref, state_ref, grad_key_ref, grad_value_ref):
    for _, i, head in head_slices(place, per_quarter, (j,)):
        rows = slice(i * DH, (i + 1) * DH)
        own = slice((j * per_quarter + i) * DH, (j * per_quarter + i + 1) * DH)
        state = state_ref[rows, :]
        grad_key = local_key_ref[:, own] + dot(value_ref[:, head], state, (1, 1))
        grad_key_ref[:, rows] = grad_key.astype(low)
        grad_value = local_value_ref[:, own] + dot(key_ref[:, head], state, (1, 0))
        grad_value_ref[:, rows] = grad_value.astype(low)


def finish_kernel(per_quarter, j, place_ref, *refs):
    finish_part(per_quarter, j, place_ref[0], *refs)


def stores(per_quarter, place, quarters, parts, outs, sems):
    width = per_quarter * DH
    copies = []
    for n, part in enumerate(parts):
        start = ((place & (QUAD - 1)) ^ quarters[n // 2]) * width
        columns = pl.ds(pl.multiple_of(start, DH), width)
        copies.append(pltpu.make_async_copy(part, outs[n % 2].at[:, columns], sems.at[n]))
    return copies


def mixed_kernel(per_quarter, quarters, place_ref, side_ref, weight_ref, other_ref, *rest):
    count = 2 * len(quarters)
    normed, parts, rest = rest[:QUAD], rest[QUAD : QUAD + count], rest[QUAD + count :]
    mixed_hbm, grad_key_hbm, grad_value_hbm, mixed_ref, sems = rest
    copies = stores(per_quarter, place_ref[0], quarters, parts, (grad_key_hbm, grad_value_hbm), sems)
    for copy in copies:
        copy.start()
    for start in range(0, other_ref.shape[1], CHUNK):
        columns = slice(start, start + CHUNK)
        total = times_weight(place_ref[0], side_ref[0], normed, weight_ref, start, CHUNK)
        mixed_ref[:, columns] = (total + other_ref[:, columns].astype(wide)).astype(low)
    copies.append(pltpu.make_async_copy(mixed_ref, mixed_hbm, sems.at[count]))
    copies[-1].start()
    for copy in copies:
        copy.wait()


def store_kernel(per_quarter, quarters, place_ref, key_ref, value_ref, local_key_ref, local_value_ref, *rest):
    suffix, before, rest = rest[:QUAD], rest[QUAD : QUAD + 2], rest[QUAD + 4 :]
    grad_key_hbm, grad_value_hbm, gain_hbm, key_part, value_part, gain_ref, sems = rest
    place = place_ref[0]
    outs = (grad_key_hbm, grad_value_hbm)
    copies = stores(per_quarter, place, quarters[:1], before, outs, sems.at[3:5])
    for copy in copies:
        copy.start()
    for j, i, head in head_slices(place, per_quarter):
        gain_ref[:, head] = pair_sum(suffix[j], per_quarter, i)
    gain_copy = pltpu.make_async_copy(gain_ref, gain_hbm, sems.at[2])
    gain_copy.start()
    finish_part(
        per_quarter, quarters[1], place, key_ref, value_ref, local_key_ref, local_value_ref, suffix[quarters[1]],
        key_part, value_part,
    )
    copies += stores(per_quarter, place, quarters[1:], (key_part, value_part), outs, sems)
    for copy in copies[2:]:
        copy.start()
    for copy in (gain_copy, *copies):
        copy.wait()


def pair_sum(ref, per_quarter, i):
    base = per_quarter * DH + 2 * i
    return ref[base : base + 1, :].astype(wide) + ref[base + 1 : base + 2, :].astype(wide)


def put_pair(ref, per_quarter, i, gain):
    base = per_quarter * DH + 2 * i
    upper = gain.astype(low)
    ref[base : base + 1, :] = upper
    ref[base + 1 : base + 2, :] = (gain - upper.astype(wide)).astype(low)


def back_kernel(side_ref, own_hbm, other_ref, weight_hbm, out_ref, weight_ref, own_ref, own_sem, sems):
    width = own_ref.shape[1]
    own = pl.ds(pl.multiple_of(side_ref[0] * width, DH), width)
    other = pl.ds(pl.multiple_of((1 - side_ref[0]) * width, DH), width)
    own_copy = pltpu.make_async_copy(own_hbm, own_ref, own_sem.at[0])
    own_copy.start()
    chunks = [slice(start, start + CHUNK) for start in range(0, weight_ref.shape[0], CHUNK)]
    copies = [
        pltpu.make_async_copy(weight_hbm.at[rows, :], weight_ref.at[rows, :], sems.at[c])
        for c, rows in enumerate(chunks)
    ]
    for copy in copies:
        copy.start()
    own_copy.wait()
    for copy, rows in zip(copies, chunks):
        copy.wait()
        total = dot(own_ref[...], weight_ref[rows, own], (1, 1))
        out_ref[:, rows] = total + dot(other_ref[...], weight_ref[rows, other], (1, 1))


def first_kernel(gains, keep, b0, b1, b2, b3, send_ref, *refs):
    rows = send_ref.shape[0] - (EXTRA if gains else 0)
    blocks = (b0, b1, b2, b3)
    total = sum(block[:rows, :].astype(wide) for block in blocks)
    send_ref[:rows, :] = total.astype(low)
    gain_refs = refs[keep:]
    if keep:
        refs[0][...] = total
    spread_gain(gains, send_ref, gain_refs, blocks, None)


def spread_gain(gains, send_ref, gain_refs, blocks, earlier):
    if not gains:
        return
    send_ref[gains * DH :, :] = jnp.zeros((EXTRA, DH), low)
    for i in range(gains):
        gain = sum(pair_sum(block, gains, i) for block in blocks)
        if earlier is not None:
            gain = gain + earlier[i : i + 1, :]
        gain_refs[0][i : i + 1, :] = gain
        put_pair(send_ref, gains, i, gain)


def is_beyond(place_ref, step, backward):
    return (place_ref[0] & step) == (0 if backward else step)


def step_kernel(gains, past, step, backward, place_ref, total_ref, got_ref, *refs):
    refs = list(refs)
    outside_ref = refs.pop(0) if past else None
    earlier = refs.pop(0) if gains else None
    total_out, outside_out, send_ref = refs[:3]
    rows = total_ref.shape[0]
    state = got_ref[:rows, :].astype(wide)
    outside = jnp.where(is_beyond(place_ref, step, backward), state, 0.0)
    outside_out[...] = outside + outside_ref[...] if past else outside
    total = total_ref[...] + state
    total_out[...] = total
    send_ref[:rows, :] = total.astype(low)
    spread_gain(gains, send_ref, refs[3:], (got_ref,), earlier)


def last_kernel(gains, past, step, backward, place_ref, b0, b1, b2, b3, got_ref, *refs):
    refs = list(refs)
    outside_ref = refs.pop(0) if past else None
    earlier = refs.pop(0) if gains else None
    blocks = (b0, b1, b2, b3)
    rows = got_ref.shape[0] - (EXTRA if gains else 0)
    outside = jnp.where(is_beyond(place_ref, step, backward), got_ref[:rows, :].astype(wide), 0.0)
    if past:
        outside = outside + outside_ref[...]
    states = [block[:rows, :].astype(wide) for block in blocks]
    pairs = (states[0] + states[1], states[2] + states[3])
    near = ((place_ref[0] & 1) != 0) != backward
    far = ((place_ref[0] & 2) != 0) != backward
    bases = (
        outside + jnp.where(far, pairs[1], 0.0),
        outside + jnp.where(far, 0.0, pairs[0]),
    )
    for j in range(QUAD):
        neighbour = states[j ^ 1]
        own = jnp.where(near, 0.0, neighbour) if j & 1 else jnp.where(near, neighbour, 0.0)
        result = bases[j >> 1] + own
        refs[j][:rows, :] = result.astype(low)
        if gains:
            refs[j][rows:, :] = jnp.zeros((EXTRA, DH), low)
    for i in range(gains):
        gain = earlier[i : i + 1, :] + pair_sum(got_ref, gains, i)
        for j in range(QUAD):
            put_pair(refs[j], gains, i, gain)


def swap(array, flip):
    count = lax.axis_size("seq")
    return lax.ppermute(array, "seq", [(i, i ^ flip) for i in range(count)])


def trade(array):
    return lax.ppermute(array, "tensor", [(0, 1), (1, 0)])


def scan(where, parts, backward, rows, gains, before_first, before_last):
    blocks, before_first = begin(parts, before_first)
    back, before_last = end(where, blocks, backward, rows, gains, before_last)
    return back, before_first, before_last


def begin(parts, before_first):
    blocks = [parts[0]] + [swap(parts[j], j) for j in range(1, QUAD)]
    return lax.optimization_barrier((blocks, before_first))


def end(where, blocks, backward, rows, gains, before_last):
    count = lax.axis_size("seq")
    total_shape = [shaped((rows, DH), wide)]
    part_shape = [shaped(blocks[0].shape, low)]
    gain_shape = [shaped((gains, DH), wide)] if gains else []
    keep = int(count > 2 * QUAD)
    send, *rest = call(
        functools.partial(first_kernel, gains, keep),
        part_shape + total_shape * keep + gain_shape,
        [VMEM] * QUAD,
    )(*blocks)
    total, gain = rest[:keep], rest[keep:]
    outside = []
    step = QUAD
    while True:
        got = swap(send, step)
        if 2 * step >= count:
            break
        new_total, new_outside, send, *gain = call(
            functools.partial(step_kernel, gains, len(outside), step, backward),
            total_shape * 2 + part_shape + gain_shape,
            [SMEM] + [VMEM] * (2 + len(outside) + len(gain)),
        )(where, *total, got, *outside, *gain)
        total, outside = [new_total], [new_outside]
        step *= 2
    got, before_last = lax.optimization_barrier((got, before_last))
    results = call(
        functools.partial(last_kernel, gains, len(outside), step, backward),
        part_shape * QUAD,
        [SMEM] + [VMEM] * (QUAD + 1 + len(outside) + len(gain)),
    )(where, *blocks, got, *outside, *gain)
    back = [results[0]] + [swap(results[j], j) for j in range(1, QUAD)]
    return back, before_last


def on_device(queries, key_vectors, values, out_weight, norm_gain, grad_output):
    tokens, width = queries.shape
    model = out_weight.shape[1]
    heads = width // DH
    per_quarter = heads // QUAD
    rows = per_quarter * DH
    place = lax.axis_index("seq")
    where = place.astype(jnp.int32).reshape(1)
    side = lax.axis_index("tensor").astype(jnp.int32).reshape(1)
    gain_row = norm_gain.reshape(1, width)
    whole = shaped((tokens, width), wide)
    whole_low = shaped((tokens, width), low)
    half = model // 2
    result_whole = pltpu.VMEM((tokens, width), low)
    one_sem = pltpu.SemaphoreType.DMA((1,))
    two_sems = pltpu.SemaphoreType.DMA((2,))

    other_grad = trade(grad_output)
    *parts, key_near, value_near = call(
        functools.partial(state_kernel, per_quarter),
        [shaped((rows, DH), low)] * QUAD + [whole_low, whole_low],
        [SMEM, HBM, HBM],
        scratch=[two_sems],
    )(where, key_vectors, values)
    squares = shaped((heads, tokens, tokens), low)
    local, query_near, scores = call(
        functools.partial(local_kernel, heads),
        [whole, whole_low, squares],
        [HBM, VMEM, VMEM],
        scratch=[one_sem],
    )(queries, key_near, value_near)
    grad_normed, weight_near = call(
        back_kernel,
        [whole, shaped(out_weight.shape, low)],
        [SMEM, HBM, VMEM, HBM],
        scratch=[
            pltpu.VMEM((tokens, half), low),
            one_sem,
            pltpu.SemaphoreType.DMA((width // CHUNK,)),
        ],
    )(side, grad_output, other_grad, out_weight)
    prefix, grad_normed, local = scan(where, parts, False, rows, 0, grad_normed, local)

    part_low = shaped((tokens, rows), low)
    normed, lows, terms = zip(
        *(
            call(
                functools.partial(norm_kernel, per_quarter, j),
                [part_low, part_low, shaped((rows + EXTRA, DH), low)],
                [SMEM, VMEM, VMEM, VMEM, FREE, VMEM],
            )(where, query_near, local, grad_normed, gain_row, prefix[j])
            for j in range(QUAD)
        )
    )
    grad_queries, sent, grad_scores = call(
        functools.partial(query_kernel, per_quarter),
        [whole_low, whole_low, squares],
        [SMEM, SMEM] + [VMEM] * (3 + 3 * QUAD),
        out_specs=[HBM, VMEM, VMEM],
        scratch=[result_whole, one_sem],
    )(where, side, key_near, value_near, weight_near, *lows, *normed, *prefix)
    blocks, sent = begin(terms, sent)
    local_pair = call(
        functools.partial(pair_kernel, per_quarter),
        [whole, whole],
        [SMEM] + [VMEM] * (3 + QUAD),
    )(where, query_near, scores, grad_scores, *lows)
    suffix, local_pair = end(where, blocks, True, rows, per_quarter, (local_pair, sent))
    local_pair, sent = local_pair
    other_part = trade(sent)
    def finish(j):
        return call(
            functools.partial(finish_kernel, per_quarter, j),
            [part_low, part_low],
            [SMEM] + [VMEM] * 5,
        )(where, key_near, value_near, *local_pair, suffix[j])

    early, late = FINISH
    finished = [part for j in early for part in finish(j)]
    mixed, grad_keys, grad_values = call(
        functools.partial(mixed_kernel, per_quarter, early),
        [whole_low, whole_low, whole_low],
        [SMEM, SMEM] + [VMEM] * (2 + QUAD + len(finished)),
        out_specs=[HBM] * 3,
        scratch=[result_whole, pltpu.SemaphoreType.DMA((len(finished) + 1,))],
    )(where, side, weight_near, other_part, *normed, *finished)
    suffix[late[0]], mixed, grad_keys, grad_values = lax.optimization_barrier(
        (suffix[late[0]], mixed, grad_keys, grad_values)
    )
    part = pltpu.VMEM((tokens, rows), low)
    grad_keys, grad_values, gain = call(
        functools.partial(store_kernel, per_quarter, late),
        [whole_low, whole_low, shaped((1, width), wide)],
        [SMEM] + [VMEM] * (6 + QUAD) + [HBM, HBM],
        out_specs=[HBM, HBM, HBM],
        scratch=[part, part, pltpu.VMEM((1, width), wide), pltpu.SemaphoreType.DMA((5,))],
        aliases={7 + QUAD: 0, 8 + QUAD: 1},
    )(where, key_near, value_near, *local_pair, *suffix, *finish(late[0]), grad_keys, grad_values)
    return mixed, grad_queries, grad_keys, grad_values, gain.reshape(width)


def solution(mesh):
    placed = (
        P(("parts", "seq"), "tensor"),
        P(("parts", "seq"), "tensor"),
        P(("parts", "seq"), "tensor"),
        P("tensor", None),
        P("tensor"),
        P(("parts", "seq"), "tensor"),
    )
    return jax.shard_map(
        on_device,
        mesh=mesh,
        in_specs=placed,
        out_specs=(
            P(("parts", "seq"), "tensor"),
            P(("parts", "seq"), "tensor"),
            P(("parts", "seq"), "tensor"),
            P(("parts", "seq"), "tensor"),
            P(("parts", "tensor")),
        ),
        check_vma=False,
    )
```
